32 devices in a mesh: rep: 2 (over x), clip: 2 (over core), strip: 8 (over z, y).
Axes of the slice: x: 2, y: 2, z: 4, core: 2. Of those that a mesh axis runs over, the one named last changes fastest.
Arguments:
- clips: bfloat16 [4, 24, 32, 6144], P(('rep', 'clip'), None, 'strip'), parts along dimension 0, may hold values from -6 to 6
- lengths: int32 [4], P(('rep', 'clip')), parts along dimension 0, may hold values from 1 to 24, as said below
- gain_in: float32 [96], replicated, may hold values from 0.1 to 1.9
- conv_in: bfloat16 [3, 3, 3, 96, 96], replicated, may hold values from -0.125 to 0.125
- bias_in: float32 [96], replicated, may hold values from -3 to 3
- gain_mid: float32 [96], replicated, may hold values from 0.1 to 1.9
- conv_mid: bfloat16 [3, 3, 3, 96, 96], replicated, may hold values from -0.125 to 0.125
- bias_mid: float32 [96], replicated, may hold values from -3 to 3
Outputs:
- encoded: bfloat16 [4, 24, 32, 6144], P(('rep', 'clip'), None, 'strip'), parts along dimension 0
The draws below stay inside these ranges and needn't reach their ends.
There are 2 independent parts, one for each index of `rep`. The reference program is written for one: setup_inputs(seed, part) draws one part's arguments, and reference() takes and returns one part's arrays. A program takes and returns all parts, laid end to end along the dimension named above; an argument that names none is the same for every part. Nothing has to cross between parts.
Inputs may be any that keep to these rules, and one draw needn't show every extreme that they name: `lengths`: clips 2k and 2k+1 form a pair; in each pair one clip has 24 frames and the other 1 to 12.
All inputs are finite; a program needn't handle non-finite values.
Results may differ from the reference program's by a relative error of at most 0.0045.
Values may be sent and summed in bfloat16 or wider, within the bound.
No kernel may reach another device: no remote copies, remote signals or barrier semaphores. Data moves between devices by JAX's collectives and lax.ppermute only.
A program may use at most 128 MiB of HBM per device.

```python
import jax
import jax.numpy as jnp
from jax import lax

C = 96
SLAB = 64
FRAMES = 24
SHORT = 12
CLIPS = 2
HEIGHT = 32


def draw_lengths(key, part):
    base = jax.random.fold_in(key, 7)
    first_key, second_key = jax.random.split(base)
    pairs = CLIPS // 2
    heavy_side = jax.random.randint(first_key, (pairs,), 0, 2)
    short_len = jax.random.randint(second_key, (pairs,), 1, SHORT + 1)
    side = jnp.arange(CLIPS) % 2
    heavy_rep = jnp.repeat(heavy_side, 2)
    short_rep = jnp.repeat(short_len, 2)
    return jnp.where(side == heavy_rep, FRAMES, short_rep).astype(jnp.int32)


def block_scale(own_key, shape, cuts, low, largest):
    level = 1.0
    for dim, shards_of in cuts:
        steps = jax.random.uniform(jax.random.fold_in(jax.random.fold_in(own_key, 6), dim), (shards_of,), jnp.float32, low / len(cuts), largest / len(cuts))
        level = level * jnp.repeat(jnp.exp(steps), shape[dim] // shards_of).reshape((-1,) + (1,) * (len(shape) - 1 - dim))
    return level


def bell_draw(key, shape, width, limit, cuts=(), held_as=jnp.bfloat16):
    gain = block_scale(key, shape, cuts, -0.22, 0.18) if cuts else 1.0
    values = jax.random.normal(key, shape, jnp.float32) * width * gain
    return jnp.minimum(jnp.maximum(values, -limit), limit).astype(held_as)


def setup_inputs(seed: int = 0, part: int = 0) -> dict:
    streams_of = jax.random.split(jax.random.key(seed), 9)
    own_keys = jax.random.split(jax.random.fold_in(streams_of[8], part), 9)
    return {
        "clips": bell_draw(own_keys[0], (CLIPS, FRAMES, HEIGHT, SLAB * C), 1.0, 6.0, ((0, 2), (2, 8))),
        "lengths": draw_lengths(jax.random.fold_in(jax.random.fold_in(streams_of[8], part), 71), part),
        "gain_in": jnp.clip(1.0 + 0.18 * jax.random.normal(streams_of[2], (C,), jnp.float32), 0.1, 1.9),
        "conv_in": bell_draw(streams_of[3], (3, 3, 3, C, C), (27 * C) ** -0.5, 0.125),
        "bias_in": bell_draw(streams_of[4], (C,), 0.5, 3.0, (), jnp.float32),
        "gain_mid": jnp.clip(1.0 + 0.18 * jax.random.normal(streams_of[5], (C,), jnp.float32), 0.1, 1.9),
        "conv_mid": bell_draw(streams_of[6], (3, 3, 3, C, C), (27 * C) ** -0.5, 0.125),
        "bias_mid": bell_draw(streams_of[7], (C,), 0.5, 3.0, (), jnp.float32),
    }


def rms_silu(values, gains):
    inverse = lax.rsqrt(lax.optimization_barrier(jnp.mean(values * values, axis=-1, keepdims=True)) + 1e-06)
    return jax.nn.silu(values * inverse * gains).astype(jnp.bfloat16)

def convolve(activity, weight):
    return lax.conv_general_dilated(activity.astype(jnp.float32), weight.astype(jnp.float32), (1, 1, 1), ((2, 0), (1, 1), (1, 1)), dimension_numbers=('NDHWC', 'DHWIO', 'NDHWC'), precision=lax.Precision.HIGHEST)

def reference(clips, lengths, gain_in, conv_in, bias_in, gain_mid, conv_mid, bias_mid):
    channels = gain_in.shape[0]
    inputs = clips.reshape(CLIPS, FRAMES, HEIGHT, SLAB, channels).astype(jnp.float32)
    first_act = rms_silu(inputs, gain_in)
    middle = (convolve(first_act, conv_in) + bias_in).astype(jnp.bfloat16)
    middle = lax.optimization_barrier(middle)
    second_act = rms_silu(middle.astype(jnp.float32), gain_mid)
    output = inputs + (convolve(second_act, conv_mid) + bias_mid)
    alive = jnp.arange(FRAMES).astype(jnp.int32)[None, :] < lengths[:, None]
    output = jnp.where(alive[:, :, None, None, None], output, jnp.zeros((), jnp.float32))
    return output.astype(jnp.bfloat16).reshape(clips.shape)
```

```python
import functools
import jax
import jax.numpy as jnp
from jax import lax
from jax.experimental import pallas as pl
from jax.experimental.pallas import tpu as pltpu
from jax.sharding import PartitionSpec as P

F32 = jnp.float32
BF16 = jnp.bfloat16


def toeplitz(weight):
    zero = jnp.zeros_like(weight[:, :, 0])
    prev = jnp.concatenate([weight[:, :, 0], zero], axis=-1)
    first = jnp.concatenate([weight[:, :, 1], weight[:, :, 0]], axis=-1)
    second = jnp.concatenate([weight[:, :, 2], weight[:, :, 1]], axis=-1)
    after = jnp.concatenate([zero, weight[:, :, 2]], axis=-1)
    rows = jnp.concatenate(
        [first, second[:, :, :32], after, prev[:, :, :32], second[:, :, 32:], prev[:, :, 32:]], axis=2
    )
    rows = jnp.concatenate([rows, rows[..., 128:]], axis=-1)
    return rows.reshape(9, 384, 256)


def pairs(vector):
    return jnp.concatenate([vector, vector, vector[32:]])[None, :]


def group_sum():
    lane = jnp.arange(256)
    column = jnp.where(lane < 96, 0, 1)
    same = column[:, None] == column[None, :]
    return jnp.where(same & (lane[:, None] < 192), 1.0, 0.0).astype(BF16)


def rms_silu(values, gains, summing):
    square = values * values
    high = square.astype(BF16)
    low = (square - high.astype(F32)).astype(BF16)
    total = jnp.dot(high, summing, preferred_element_type=F32) + jnp.dot(
        low, summing, preferred_element_type=F32
    )
    inverse = lax.rsqrt(total * (1.0 / 96.0) + 1e-06)
    scaled = values * inverse * gains
    return scaled / (1.0 + jnp.exp(-scaled))


def shift_down(block):
    row = lax.broadcasted_iota(jnp.int32, block.shape, block.ndim - 2)
    return jnp.where(row == 0, 0.0, jnp.roll(block, 1, axis=-2))


def shift_up(block):
    row = lax.broadcasted_iota(jnp.int32, block.shape, block.ndim - 2)
    return jnp.where(row == block.shape[-2] - 1, 0.0, jnp.roll(block, -1, axis=-2))


def store_windows(ref, frame, act):
    even0, even1 = act[:, 0, :, :128], act[:, 0, :, 128:]
    odd0, odd1 = act[:, 1, :, :128], act[:, 1, :, 128:]
    lane = lax.broadcasted_iota(jnp.int32, even0.shape, even0.ndim - 1)
    mix = jnp.where(lane < 96, odd0, shift_down(odd0))
    tail = jnp.where(lane < 64, even1, shift_down(odd1))
    ref[frame, :, 0, :, 0:128] = even0.astype(BF16)
    ref[frame, :, 0, :, 128:256] = mix.astype(BF16)
    ref[frame, :, 0, :, 256:384] = tail.astype(BF16)
    mix = jnp.where(lane < 96, shift_up(even0), even0)
    tail = jnp.where(lane < 64, odd1, even1)
    ref[frame, :, 1, :, 0:128] = odd0.astype(BF16)
    ref[frame, :, 1, :, 128:256] = mix.astype(BF16)
    ref[frame, :, 1, :, 256:384] = tail.astype(BF16)


def to_pairs(quad):
    x0, x1, x2 = quad[..., :128], quad[..., 128:256], quad[..., 256:]
    r1 = jnp.roll(x1, 64, axis=-1)
    r2 = jnp.roll(x2, 64, axis=-1)
    lane = lax.broadcasted_iota(jnp.int32, x0.shape, x0.ndim - 1)
    low = lane < 64
    even = jnp.concatenate([x0, jnp.where(low, x1, r1)], axis=-1)
    odd = jnp.concatenate([jnp.where(low, r1, r2), jnp.where(low, r2, x2)], axis=-1)
    return jnp.stack([even, odd], axis=1)


def from_pairs(both):
    even0, even1 = both[:, 0, :, :128], both[:, 0, :, 128:]
    odd0, odd1 = both[:, 1, :, :128], both[:, 1, :, 128:]
    turned = jnp.roll(odd0, 64, axis=-1)
    lane = lax.broadcasted_iota(jnp.int32, even0.shape, even0.ndim - 1)
    low = lane < 64
    return jnp.concatenate([even0, jnp.where(low, even1, turned), jnp.where(low, turned, odd1)], axis=-1)


def conv(ref, weight_ref, start, frames, rows):
    total = None
    for lag in range(3):
        for row in range(3):
            window = ref[pl.ds(start + lag, frames), row : row + rows]
            window = window.reshape(frames * rows * 32, 384)
            part = jnp.dot(window, weight_ref[3 * lag + row], preferred_element_type=F32)
            total = part if total is None else total + part
    return total


def body(
    step_frames, own_rows, info, own, top, low, w1, w2, gain1, bias1, gain2, bias2, summing, out,
    first_ref, second_ref, acc_ref,
):
    step = pl.program_id(0)
    length = info[0]
    start = step * step_frames
    rows1 = own_rows + 2

    @pl.when(step == 0)
    def _():
        first_ref[0:2] = jnp.zeros_like(first_ref[0:2])
        second_ref[0:2] = jnp.zeros_like(second_ref[0:2])

    @pl.when(start >= length)
    def _():
        out[...] = jnp.zeros_like(out)

    @pl.when(start < length)
    def _():
        for t in range(step_frames):
            for piece, at in ((top, 0), (own, 2), (low, 2 + own_rows)):
                count = piece.shape[1]
                values = to_pairs(piece[t].astype(F32))
                act = rms_silu(values.reshape(count * 32, 256), gain1[...], summing[...])
                store_windows(first_ref.at[:, at : at + count], start + t + 2, act.reshape(count, 2, 16, 256))
        acc_ref[...] = conv(first_ref, w1, start, step_frames, rows1)
        for t in range(step_frames):
            middle = acc_ref[t * rows1 * 32 : (t + 1) * rows1 * 32] + bias1[...]
            middle = middle.astype(BF16).astype(F32)
            act = rms_silu(middle, gain2[...], summing[...])
            act = act.reshape(rows1, 2, 16, 256)
            keep0 = info[1].astype(F32)
            keep1 = info[2].astype(F32)
            act = jnp.concatenate([act[:1] * keep0, act[1:-1], act[-1:] * keep1], axis=0)
            store_windows(second_ref, start + t + 2, act)
        size = step_frames * own_rows * 32
        acc_ref[0:size] = conv(second_ref, w2, start, step_frames, own_rows)
        for t in range(step_frames):
            branch = acc_ref[t * own_rows * 32 : (t + 1) * own_rows * 32] + bias2[...]
            branch = from_pairs(branch.reshape(own_rows, 2, 16, 256))
            total = own[t].astype(F32) + branch
            total = jnp.where(start + t < length, total, 0.0)
            out[t] = total.astype(BF16)


def block(info, own, top, low, w1, w2, gain1, bias1, gain2, bias2, summing, step_frames):
    frames, own_rows = own.shape[:2]

    def full(a):
        return pl.BlockSpec(a.shape, lambda i: (0,) * a.ndim, pipeline_mode=pl.Buffered(1))

    def chunk(a):
        return pl.BlockSpec((step_frames,) + a.shape[1:], lambda i: (i, 0, 0, 0))

    return pl.pallas_call(
        functools.partial(body, step_frames, own_rows),
        grid=(frames // step_frames,),
        out_shape=jax.ShapeDtypeStruct(own.shape, BF16),
        in_specs=[
            pl.BlockSpec(memory_space=pltpu.SMEM),
            chunk(own), chunk(top), chunk(low),
            full(w1), full(w2), full(gain1), full(bias1), full(gain2), full(bias2), full(summing),
        ],
        out_specs=chunk(own),
        scratch_shapes=[
            pltpu.VMEM((frames + 2, own_rows + 4, 2, 16, 384), BF16),
            pltpu.VMEM((frames + 2, own_rows + 2, 2, 16, 384), BF16),
            pltpu.VMEM((step_frames * (own_rows + 2) * 32, 256), F32),
        ],
        compiler_params=pltpu.CompilerParams(dimension_semantics=("arbitrary",), vmem_limit_bytes=60 << 20),
    )(info, own, top, low, w1, w2, gain1, bias1, gain2, bias2, summing)


STEP = 4


def local(clips, lengths, gain_in, conv_in, bias_in, gain_mid, conv_mid, bias_mid):
    own = clips[0].reshape(clips.shape[1], clips.shape[2], 16, 384)
    count = lax.axis_size("strip")
    place = lax.axis_index("strip")
    forward = [(i, i + 1) for i in range(count - 1)]
    backward = [(i + 1, i) for i in range(count - 1)]
    top = lax.ppermute(own[:, -2:], "strip", forward)
    low = lax.ppermute(own[:, :2], "strip", backward)
    info = jnp.stack(
        [lengths[0], (place > 0).astype(jnp.int32), (place < count - 1).astype(jnp.int32)]
    )
    out = block(
        info, own, top, low, toeplitz(conv_in), toeplitz(conv_mid),
        pairs(gain_in), pairs(bias_in), pairs(gain_mid), pairs(bias_mid), group_sum(), STEP,
    )
    return out.reshape(clips.shape)


def solution(mesh):
    data = P(("rep", "clip"), None, "strip", None)
    in_specs = (data, P(("rep", "clip")), P(), P(), P(), P(), P(), P())
    return jax.shard_map(local, mesh=mesh, in_specs=in_specs, out_specs=data, check_vma=False)
```

```python
import functools

import jax
import jax.numpy as jnp
from jax import lax
from jax.experimental import pallas as pl
from jax.experimental.pallas import tpu as pltpu
from jax.sharding import PartitionSpec as P

F32 = jnp.float32
BF16 = jnp.bfloat16
SHORT = 12
PARTS = 4
SCALE = 0.5 * 96.0**0.5


def toeplitz(weight):
    zero = jnp.zeros_like(weight[:, :, 0])
    prev = jnp.concatenate([weight[:, :, 0], zero], axis=-1)
    first = jnp.concatenate([weight[:, :, 1], weight[:, :, 0]], axis=-1)
    second = jnp.concatenate([weight[:, :, 2], weight[:, :, 1]], axis=-1)
    after = jnp.concatenate([zero, weight[:, :, 2]], axis=-1)
    rows = jnp.concatenate(
        [first, second[:, :, :32], after, prev[:, :, :32], second[:, :, 32:], prev[:, :, 32:]], axis=2
    )
    rows = jnp.concatenate([rows, rows[..., 128:]], axis=-1)
    return rows.reshape(9 * 384, 256)


def pairs(vector):
    return jnp.concatenate([vector, vector, vector[32:]])[None, :]


def group_sum():
    lane = jnp.arange(256)
    column = jnp.where(lane < 96, 0, 1)
    same = column[:, None] == column[None, :]
    return jnp.where(same & (lane[:, None] < 192), 1.0, 0.0).astype(BF16)


def rms_silu(values, gains, summing):
    narrow = (values * values).astype(BF16)
    total = jnp.dot(narrow, summing, preferred_element_type=F32)
    half = values * (lax.rsqrt(total + 96e-06) * gains)
    return half + half * jnp.tanh(half)


def shift_down(block):
    row = lax.broadcasted_iota(jnp.int32, block.shape, block.ndim - 2)
    return jnp.where(row == 0, 0.0, jnp.roll(block, 1, axis=-2))


def shift_up(block):
    row = lax.broadcasted_iota(jnp.int32, block.shape, block.ndim - 2)
    return jnp.where(row == block.shape[-2] - 1, 0.0, jnp.roll(block, -1, axis=-2))


def store_windows(ref, frame, act):
    even0, even1 = act[:, 0, :, :128], act[:, 0, :, 128:]
    odd0, odd1 = act[:, 1, :, :128], act[:, 1, :, 128:]
    lane = lax.broadcasted_iota(jnp.int32, even0.shape, even0.ndim - 1)
    mix = jnp.where(lane < 96, odd0, shift_down(odd0))
    tail = jnp.where(lane < 64, even1, shift_down(odd1))
    ref[frame, :, 0, :, 0:128] = even0.astype(BF16)
    ref[frame, :, 0, :, 128:256] = mix.astype(BF16)
    ref[frame, :, 0, :, 256:384] = tail.astype(BF16)
    mix = jnp.where(lane < 96, shift_up(even0), even0)
    tail = jnp.where(lane < 64, odd1, even1)
    ref[frame, :, 1, :, 0:128] = odd0.astype(BF16)
    ref[frame, :, 1, :, 128:256] = mix.astype(BF16)
    ref[frame, :, 1, :, 256:384] = tail.astype(BF16)


def to_pairs(quad):
    x0, x1, x2 = quad[..., :128], quad[..., 128:256], quad[..., 256:]
    r1 = jnp.roll(x1, 64, axis=-1)
    r2 = jnp.roll(x2, 64, axis=-1)
    lane = lax.broadcasted_iota(jnp.int32, x0.shape, x0.ndim - 1)
    low = lane < 64
    even = jnp.concatenate([x0, jnp.where(low, x1, r1)], axis=-1)
    odd = jnp.concatenate([jnp.where(low, r1, r2), jnp.where(low, r2, x2)], axis=-1)
    return jnp.stack([even, odd], axis=1)


def from_pairs(both):
    even0, even1 = both[:, 0, :, :128], both[:, 0, :, 128:]
    odd0, odd1 = both[:, 1, :, :128], both[:, 1, :, 128:]
    turned = jnp.roll(odd0, 64, axis=-1)
    lane = lax.broadcasted_iota(jnp.int32, even0.shape, even0.ndim - 1)
    low = lane < 64
    return jnp.concatenate([even0, jnp.where(low, even1, turned), jnp.where(low, turned, odd1)], axis=-1)


def conv(ref, weight_ref, acc_ref, frames, rows):
    weight = weight_ref[...]
    each = rows // 2
    size = frames * each * 32
    for part in range(2):
        windows = []
        for lag in range(3):
            for row in range(3):
                at = part * each + row
                windows.append(ref[lag : lag + frames, at : at + each].reshape(size, 384))
        acc_ref[part] = jnp.dot(
            jnp.concatenate(windows, axis=1), weight, preferred_element_type=F32
        ).reshape(frames, each, 32, 256)


def body(base, frames, own_rows, quads, halo_at, *refs):
    info, own = refs[:2]
    halos = refs[2 : 2 + len(set(k for pair in halo_at for k, _, _ in pair))]
    at = 2 + len(halos)
    w1, w2, gain1, bias1, gain2, bias2, summing = refs[at : at + 7]
    at += 7
    carried = refs[at : at + 3] if base else None
    at += 3 if base else 0
    out, carry1, carry2, first_ref, second_ref, acc1, acc2, lines_ref = refs[at:]
    length = info[0]
    rows1 = own_rows + 2
    rows0 = own_rows + 4

    @pl.when(base >= length)
    def _():
        out[...] = jnp.zeros_like(out)

    @pl.when(base < length)
    def _():
        if base:
            first_ref[0:2] = carried[1][...]
            second_ref[0:2] = carried[2][...]
        else:
            first_ref[0:2] = jnp.zeros_like(first_ref[0:2])
            second_ref[0:2] = jnp.zeros_like(second_ref[0:2])
        for t in range(frames):
            slot = t % 2
            (top_k, top_t, top_r), (low_k, low_t, low_r) = halo_at[t]
            pieces = (
                (halos[top_k][top_t, top_r : top_r + 2].astype(F32), 0, 2),
                (own[t].astype(F32), 2, own_rows),
                (halos[low_k][low_t, low_r : low_r + 2].astype(F32), 2 + own_rows, 2),
            )
            for values, where, count in pieces:
                for q in range(quads):
                    for v in range(3):
                        lane = (3 * q + v) * 128
                        lines_ref[slot, v, pl.ds(where * quads + q, count, stride=quads)] = values[
                            :, lane : lane + 128
                        ]
            quad = jnp.concatenate([lines_ref[slot, v] for v in range(3)], axis=1).reshape(rows0, quads, 384)
            act = rms_silu(to_pairs(quad).reshape(rows0 * 32, 256), gain1[...], summing[...])
            store_windows(first_ref, t + 2, act.reshape(rows0, 2, 16, 256))
        carry1[...] = first_ref[frames : frames + 2]
        conv(first_ref, w1, acc1, frames, rows1)
        keep0 = info[1].astype(F32)
        keep1 = info[2].astype(F32)
        for t in range(frames):
            middle = jnp.concatenate([acc1[0, t], acc1[1, t]], axis=0).reshape(rows1 * 32, 256)
            middle = (middle + bias1[...]).astype(BF16).astype(F32)
            act = rms_silu(middle, gain2[...], summing[...]).reshape(rows1, 2, 16, 256)
            act = jnp.concatenate([act[:1] * keep0, act[1:-1], act[-1:] * keep1], axis=0)
            store_windows(second_ref, t + 2, act)
        carry2[...] = second_ref[frames : frames + 2]
        conv(second_ref, w2, acc2, frames, own_rows)
        for t in range(frames):
            slot = t % 2
            branch = jnp.concatenate([acc2[0, t], acc2[1, t]], axis=0).reshape(own_rows * 32, 256)
            branch = from_pairs((branch + bias2[...]).reshape(own_rows, 2, 16, 256))
            branch = branch.reshape(own_rows * quads, 384)
            for v in range(3):
                lines_ref[slot, v, 0 : own_rows * quads] = branch[:, v * 128 : v * 128 + 128]
            pieces = []
            for q in range(quads):
                for v in range(3):
                    pieces.append(lines_ref[slot, v, pl.ds(q, own_rows, stride=quads)])
            total = own[t].astype(F32) + jnp.concatenate(pieces, axis=1)
            out[t] = jnp.where(base + t < length, total, 0.0).astype(BF16)


def whole(array):
    return pl.BlockSpec(array.shape, lambda i: (0,) * array.ndim, pipeline_mode=pl.Buffered(1))


def stage(base, frames, info, own, halos, halo_at, consts, carried):
    own_rows, width = own.shape[1:]
    quads = width // 384
    index = base // frames
    block = pl.BlockSpec((frames, own_rows, width), lambda i: (index, 0, 0), pipeline_mode=pl.Buffered(1))
    rows1, rows0 = own_rows + 2, own_rows + 4
    carry = [
        jax.ShapeDtypeStruct((2, rows0, 2, quads, 384), BF16),
        jax.ShapeDtypeStruct((2, rows1, 2, quads, 384), BF16),
    ]
    operands = [info, own, *halos, *consts]
    in_specs = [pl.BlockSpec(memory_space=pltpu.SMEM), block]
    in_specs += [whole(a) for a in (*halos, *consts)]
    aliases = {}
    if base:
        aliases = {len(operands): 0}
        operands += list(carried)
        in_specs += [pl.BlockSpec(memory_space=pl.ANY)] + [whole(a) for a in carry]
    return pl.pallas_call(
        functools.partial(body, base, frames, own_rows, quads, halo_at),
        grid=(1,),
        out_shape=[jax.ShapeDtypeStruct(own.shape, BF16)] + carry,
        in_specs=in_specs,
        out_specs=[block] + [whole(a) for a in carry],
        scratch_shapes=[
            pltpu.VMEM((frames + 2, rows0, 2, quads, 384), BF16),
            pltpu.VMEM((frames + 2, rows1, 2, quads, 384), BF16),
            pltpu.VMEM((2, frames, rows1 // 2, 32, 256), F32),
            pltpu.VMEM((2, frames, own_rows // 2, 32, 256), F32),
            pltpu.VMEM((2, 3, rows0 * quads, 128), F32),
        ],
        input_output_aliases=aliases,
        compiler_params=pltpu.CompilerParams(
            dimension_semantics=("arbitrary",), vmem_limit_bytes=VMEM_LIMIT
        ),
        cost_estimate=pl.CostEstimate(
            flops=2 * frames * 10 * 32 * 3456 * 256, bytes_accessed=6 << 20, transcendentals=0
        ),
        name=f"stage{index}",
    )(*operands)


VMEM_LIMIT = 28 << 20


def local(clips, lengths, gain_in, conv_in, bias_in, gain_mid, conv_mid, bias_mid):
    own = clips[0]
    frames = own.shape[0]
    part = frames // PARTS
    half = part // 2
    count = lax.axis_size("strip")
    place = lax.axis_index("strip")
    forward = [(i, i + 1) for i in range(count - 1)]
    backward = [(i + 1, i) for i in range(count - 1)]
    swap = [(i, i ^ 1) for i in range(lax.axis_size("clip"))]

    def edges(block):
        top = lax.ppermute(block[:, -2:], "strip", forward)
        low = lax.ppermute(block[:, :2], "strip", backward)
        return top, low

    halos = []
    for index in range(SHORT // part):
        halos.append(edges(own[index * part : (index + 1) * part]))
    heavy = lengths[0] > SHORT
    late = range(SHORT, frames, part)
    lent = lax.ppermute(
        jnp.concatenate([own[at + half : at + part] for at in late], axis=0), "clip", swap
    )
    for index, at in enumerate(late):
        sent = jnp.where(heavy, own[at : at + half], lent[index * half : (index + 1) * half])
        top, low = edges(sent)
        back = lax.ppermute(jnp.concatenate([top, low], axis=1), "clip", swap)
        halos.append((top, low, back))
    info = jnp.stack(
        [lengths[0], (place > 0).astype(jnp.int32), (place < count - 1).astype(jnp.int32)]
    )
    consts = (
        toeplitz(conv_in), toeplitz(conv_mid), SCALE * pairs(gain_in), pairs(bias_in),
        SCALE * pairs(gain_mid), pairs(bias_mid), group_sum(),
    )
    carried = None
    for index in range(PARTS):
        if len(halos[index]) == 2:
            halo_at = tuple(((0, t, 0), (1, t, 0)) for t in range(part))
        else:
            halo_at = tuple(((0, t, 0), (1, t, 0)) for t in range(half))
            halo_at += tuple(((2, t, 0), (2, t, 2)) for t in range(half))
        carried = stage(index * part, part, info, own, halos[index], halo_at, consts, carried)
    return carried[0][None]


def solution(mesh):
    data = P(("rep", "clip"), None, "strip", None)
    in_specs = (data, P(("rep", "clip")), P(), P(), P(), P(), P(), P())
    return jax.shard_map(local, mesh=mesh, in_specs=in_specs, out_specs=data, check_vma=False)
```

```python
import functools

import jax
import jax.numpy as jnp
from jax import lax
from jax.experimental import pallas as pl
from jax.experimental.pallas import tpu as pltpu
from jax.sharding import PartitionSpec as P

F32 = jnp.float32
BF16 = jnp.bfloat16
SHORT = 12
PARTS = 3
SCALE = 0.5 * 96.0**0.5


def spread_weight(raw_ref, out_ref):
    def tap(index, _):
        lag, row = index // 3, index % 3
        w0 = raw_ref[lag, row, 0].astype(F32)
        w1 = raw_ref[lag, row, 1].astype(F32)
        w2 = raw_ref[lag, row, 2].astype(F32)
        zero = jnp.zeros_like(w0)
        first = twice(w1, w0).astype(BF16)
        second = twice(w2, w1).astype(BF16)
        after = twice(zero, w2).astype(BF16)
        prev = twice(w0, zero).astype(BF16)
        base = index * 384
        out_ref[pl.ds(base, 96)] = first
        out_ref[pl.ds(base + 96, 32)] = second[:32]
        out_ref[pl.ds(base + 128, 96)] = after
        out_ref[pl.ds(base + 224, 32)] = prev[:32]
        out_ref[pl.ds(base + 256, 64)] = second[32:]
        out_ref[pl.ds(base + 320, 64)] = prev[32:]
        return 0

    lax.fori_loop(0, 9, tap, 0)


def twice(left, right):
    return jnp.concatenate([left, right, right[:, 32:]], axis=1)


def group_sum():
    row = lax.broadcasted_iota(jnp.int32, (256, 256), 0)
    column = lax.broadcasted_iota(jnp.int32, (256, 256), 1)
    same = (row < 96) == (column < 96)
    return jnp.where(same & (row < 192), 1.0, 0.0).astype(BF16)


def rms_silu(values, gains, summing):
    narrow = (values * values).astype(BF16)
    total = jnp.dot(narrow, summing, preferred_element_type=F32)
    half = values * (lax.rsqrt(total + 96e-06) * gains)
    return half + half * jnp.tanh(half)


def shift_down(block):
    row = lax.broadcasted_iota(jnp.int32, block.shape, block.ndim - 2)
    return jnp.where(row == 0, 0.0, jnp.roll(block, 1, axis=-2))


def shift_up(block):
    row = lax.broadcasted_iota(jnp.int32, block.shape, block.ndim - 2)
    return jnp.where(row == block.shape[-2] - 1, 0.0, jnp.roll(block, -1, axis=-2))


def store_windows(ref, frame, act):
    even0, even1 = act[:, 0, :, :128], act[:, 0, :, 128:]
    odd0, odd1 = act[:, 1, :, :128], act[:, 1, :, 128:]
    lane = lax.broadcasted_iota(jnp.int32, even0.shape, even0.ndim - 1)
    mix = jnp.where(lane < 96, odd0, shift_down(odd0))
    tail = jnp.where(lane < 64, even1, shift_down(odd1))
    ref[frame, :, 0, :, 0:128] = even0.astype(BF16)
    ref[frame, :, 0, :, 128:256] = mix.astype(BF16)
    ref[frame, :, 0, :, 256:384] = tail.astype(BF16)
    mix = jnp.where(lane < 96, shift_up(even0), even0)
    tail = jnp.where(lane < 64, odd1, even1)
    ref[frame, :, 1, :, 0:128] = odd0.astype(BF16)
    ref[frame, :, 1, :, 128:256] = mix.astype(BF16)
    ref[frame, :, 1, :, 256:384] = tail.astype(BF16)


def to_pairs(quad):
    x0, x1, x2 = quad[..., :128], quad[..., 128:256], quad[..., 256:]
    r1 = jnp.roll(x1, 64, axis=-1)
    r2 = jnp.roll(x2, 64, axis=-1)
    lane = lax.broadcasted_iota(jnp.int32, x0.shape, x0.ndim - 1)
    low = lane < 64
    even = jnp.concatenate([x0, jnp.where(low, x1, r1)], axis=-1)
    odd = jnp.concatenate([jnp.where(low, r1, r2), jnp.where(low, r2, x2)], axis=-1)
    return jnp.stack([even, odd], axis=1)


def from_pairs(both):
    even0, even1 = both[:, 0, :, :128], both[:, 0, :, 128:]
    odd0, odd1 = both[:, 1, :, :128], both[:, 1, :, 128:]
    turned = jnp.roll(odd0, 64, axis=-1)
    lane = lax.broadcasted_iota(jnp.int32, even0.shape, even0.ndim - 1)
    low = lane < 64
    return jnp.concatenate([even0, jnp.where(low, even1, turned), jnp.where(low, turned, odd1)], axis=-1)


def to_quads(values, lines_ref, slot, where, quads):
    count = values.shape[0]
    for q in range(quads):
        for v in range(3):
            lane = (3 * q + v) * 128
            lines_ref[slot, v, pl.ds(where * quads + q, count, stride=quads)] = values[:, lane : lane + 128]


def read_quads(lines_ref, slot, rows, quads):
    parts = [lines_ref[slot, v, 0 : rows * quads] for v in range(3)]
    return jnp.concatenate(parts, axis=1).reshape(rows, quads, 384)


def windows_dot(ref, weight, start, frames, row, count):
    windows = []
    for lag in range(3):
        for step in range(3):
            at = row + step
            windows.append(ref[start + lag : start + lag + frames, at : at + count].reshape(frames * count * 32, 384))
    product = jnp.dot(jnp.concatenate(windows, axis=1), weight, preferred_element_type=F32)
    return product.reshape(frames, count, 32, 256)


def prepare(
    own, raw1, raw2, gain1, bias1, gain2, bias2, w1, w2, vectors, first, second, acc, lines_ref
):
    frames, own_rows, width = own.shape
    quads = width // 384
    inner = own_rows - 2
    spread_weight(raw1, w1)
    spread_weight(raw2, w2)
    for index, (source, scale) in enumerate(((gain1, SCALE), (bias1, 1.0), (gain2, SCALE), (bias2, 1.0))):
        line = source[...] * scale
        vectors[index : index + 1] = twice(line, line)
    summing = group_sum()
    first[0:2] = jnp.zeros_like(first[0:2])
    second[0:2] = jnp.zeros_like(second[0:2])

    def one(t, slot):
        to_quads(own[t].astype(F32), lines_ref, slot, 0, quads)
        quad = read_quads(lines_ref, slot, own_rows, quads)
        act = rms_silu(to_pairs(quad).reshape(own_rows * 32, 256), vectors[0:1], summing)
        store_windows(first, t + 2, act.reshape(own_rows, 2, 16, 256))

    def act1(step, _):
        for slot in range(UNROLL):
            one(step * UNROLL + slot, slot)
        return 0

    lax.fori_loop(0, frames // UNROLL, act1, 0)
    weight = w1[...]
    for row in range(inner):
        acc[row] = windows_dot(first, weight, 0, frames, row, 1)

    def act2(step, _):
        for slot in range(UNROLL):
            t = step * UNROLL + slot
            middle = jnp.concatenate([acc[row, t] for row in range(inner)], axis=0)
            middle = (middle.reshape(inner * 32, 256) + vectors[1:2]).astype(BF16).astype(F32)
            act = rms_silu(middle, vectors[2:3], summing)
            store_windows(second, t + 2, act.reshape(inner, 2, 16, 256))
        return 0

    lax.fori_loop(0, frames // UNROLL, act2, 0)


def body(base, frames, own_rows, quads, count, *refs):
    lengths, own, near, far, w1, w2, vectors, first, second = refs[:9]
    carried = refs[9:12] if base else None
    out, carry1, carry2, first_ref, second_ref, acc1, acc2, lines_ref = refs[12 if base else 9 :]
    length = lengths[0]
    place = lax.axis_index("strip")
    odd = place % 2 == 1
    rows1 = own_rows + 2
    rows0 = own_rows + 4

    @pl.when(base >= length)
    def _():
        out[...] = jnp.zeros_like(out)

    @pl.when(base < length)
    def _():
        first_ref[:, 2 : 2 + own_rows] = first[...]
        second_ref[:, 2:own_rows] = second[...]
        if base:
            first_ref[0:2, 0:2] = carried[1][:, 0:2]
            first_ref[0:2, 2 + own_rows :] = carried[1][:, 2:4]
            second_ref[0:2, 0:2] = carried[2][:, 0:2]
            second_ref[0:2, own_rows:] = carried[2][:, 2:4]
        else:
            first_ref[0:2, 0:2] = jnp.zeros_like(first_ref[0:2, 0:2])
            first_ref[0:2, 2 + own_rows :] = jnp.zeros_like(first_ref[0:2, 0:2])
            second_ref[0:2, 0:2] = jnp.zeros_like(second_ref[0:2, 0:2])
            second_ref[0:2, own_rows:] = jnp.zeros_like(second_ref[0:2, 0:2])
        summing = group_sum()
        for t in range(frames):
            slot = t % UNROLL
            left, right = near[t].astype(F32), far[t].astype(F32)
            to_quads(jnp.where(odd, left, right), lines_ref, slot, 0, quads)
            to_quads(jnp.where(odd, right, left), lines_ref, slot, 2, quads)
            quad = read_quads(lines_ref, slot, 4, quads)
            act = rms_silu(to_pairs(quad).reshape(4 * 32, 256), vectors[0:1], summing)
            act = act.reshape(4, 2, 16, 256)
            store_windows(first_ref.at[:, 0:2], t + 2, act[:2])
            store_windows(first_ref.at[:, 2 + own_rows :], t + 2, act[2:])
        carry1[:, 0:2] = first_ref[frames : frames + 2, 0:2]
        carry1[:, 2:4] = first_ref[frames : frames + 2, 2 + own_rows :]
        weight = w1[...]
        acc1[0] = windows_dot(first_ref, weight, 0, frames, 0, 2)
        acc1[1] = windows_dot(first_ref, weight, 0, frames, own_rows, 2)
        above = (place > 0).astype(F32)
        below = (place < count - 1).astype(F32)
        for t in range(frames):
            middle = jnp.concatenate([acc1[0, t], acc1[1, t]], axis=0).reshape(4 * 32, 256)
            middle = (middle + vectors[1:2]).astype(BF16).astype(F32)
            act = rms_silu(middle, vectors[2:3], summing).reshape(4, 2, 16, 256)
            store_windows(second_ref.at[:, 0:2], t + 2, jnp.concatenate([act[0:1] * above, act[1:2]], axis=0))
            store_windows(second_ref.at[:, own_rows:], t + 2, jnp.concatenate([act[2:3], act[3:4] * below], axis=0))
        carry2[:, 0:2] = second_ref[frames : frames + 2, 0:2]
        carry2[:, 2:4] = second_ref[frames : frames + 2, own_rows:]
        weight = w2[...]
        each = own_rows // 2
        acc2[0] = windows_dot(second_ref, weight, 0, frames, 0, each)
        acc2[1] = windows_dot(second_ref, weight, 0, frames, each, each)
        for t in range(frames):
            slot = t % UNROLL
            branch = jnp.concatenate([acc2[0, t], acc2[1, t]], axis=0).reshape(own_rows * 32, 256)
            branch = from_pairs((branch + vectors[3:4]).reshape(own_rows, 2, 16, 256))
            branch = branch.reshape(own_rows * quads, 384)
            for v in range(3):
                lines_ref[slot, v, 0 : own_rows * quads] = branch[:, v * 128 : v * 128 + 128]
            pieces = []
            for q in range(quads):
                for v in range(3):
                    pieces.append(lines_ref[slot, v, pl.ds(q, own_rows, stride=quads)])
            total = own[t].astype(F32) + jnp.concatenate(pieces, axis=1)
            out[t] = jnp.where(base + t < length, total, 0.0).astype(BF16)


UNROLL = 2
VMEM_LIMIT = 30 << 20


def whole(array):
    return pl.BlockSpec(array.shape, lambda i: (0,) * len(array.shape), pipeline_mode=pl.Buffered(1))


def prepare_call(own, raw1, raw2, gain1, bias1, gain2, bias2):
    frames, own_rows, width = own.shape
    quads = width // 384
    results = [
        jax.ShapeDtypeStruct((3456, 256), BF16),
        jax.ShapeDtypeStruct((3456, 256), BF16),
        jax.ShapeDtypeStruct((8, 256), F32),
        jax.ShapeDtypeStruct((frames + 2, own_rows, 2, quads, 384), BF16),
        jax.ShapeDtypeStruct((frames + 2, own_rows - 2, 2, quads, 384), BF16),
    ]
    operands = (own, raw1, raw2, gain1, bias1, gain2, bias2)
    return pl.pallas_call(
        prepare,
        grid=(1,),
        out_shape=results,
        in_specs=[whole(a) for a in operands],
        out_specs=[whole(a) for a in results],
        scratch_shapes=[
            pltpu.VMEM((own_rows - 2, frames, 1, 32, 256), F32),
            pltpu.VMEM((UNROLL, 3, own_rows * quads, 128), F32),
        ],
        compiler_params=pltpu.CompilerParams(
            dimension_semantics=("arbitrary",), vmem_limit_bytes=VMEM_LIMIT
        ),
        cost_estimate=pl.CostEstimate(
            flops=2 * frames * 2 * 32 * 3456 * 256, bytes_accessed=8 << 20, transcendentals=0
        ),
        name="prepare",
    )(*operands)


def stage(base, frames, count, lengths, own, near, far, prepared, carried):
    own_rows, width = own.shape[1:]
    quads = width // 384
    index = base // frames

    def block(array):
        return pl.BlockSpec(
            (frames,) + array.shape[1:],
            lambda i: (index,) + (0,) * (array.ndim - 1),
            pipeline_mode=pl.Buffered(1),
        )

    def lagged(array):
        rest = array.shape[1:]
        return pl.BlockSpec(
            (pl.Element(frames + 2),) + tuple(pl.Element(n) for n in rest),
            lambda i: (base,) + (0,) * len(rest),
            pipeline_mode=pl.Buffered(1),
        )

    w1, w2, vectors, first, second = prepared
    rows1, rows0 = own_rows + 2, own_rows + 4
    carry = [jax.ShapeDtypeStruct((2, 4, 2, quads, 384), BF16)] * 2
    operands = [lengths, own, near, far, w1, w2, vectors, first, second]
    in_specs = [pl.BlockSpec(memory_space=pltpu.SMEM), block(own)]
    in_specs += [whole(a) for a in (near, far, w1, w2, vectors)] + [lagged(first), lagged(second)]
    aliases = {}
    if base:
        aliases = {len(operands): 0}
        operands += list(carried)
        in_specs += [pl.BlockSpec(memory_space=pl.ANY)] + [whole(a) for a in carry]
    return pl.pallas_call(
        functools.partial(body, base, frames, own_rows, quads, count),
        grid=(1,),
        out_shape=[jax.ShapeDtypeStruct(own.shape, BF16)] + carry,
        in_specs=in_specs,
        out_specs=[block(own)] + [whole(a) for a in carry],
        scratch_shapes=[
            pltpu.VMEM((frames + 2, rows0, 2, quads, 384), BF16),
            pltpu.VMEM((frames + 2, rows1, 2, quads, 384), BF16),
            pltpu.VMEM((2, frames, 2, 32, 256), F32),
            pltpu.VMEM((2, frames, own_rows // 2, 32, 256), F32),
            pltpu.VMEM((UNROLL, 3, 4 * quads, 128), F32),
        ],
        input_output_aliases=aliases,
        compiler_params=pltpu.CompilerParams(
            dimension_semantics=("arbitrary",), vmem_limit_bytes=VMEM_LIMIT
        ),
        cost_estimate=pl.CostEstimate(
            flops=2 * frames * 8 * 32 * 3456 * 256, bytes_accessed=6 << 20, transcendentals=0
        ),
        name=f"stage{index}",
    )(*operands)


def local(clips, lengths, gain_in, conv_in, bias_in, gain_mid, conv_mid, bias_mid):
    own = clips[0]
    frames, own_rows = own.shape[:2]
    part = frames // PARTS
    count = lax.axis_size("strip")
    odd = lax.axis_index("strip") % 2 == 1
    near_route = [(i, i ^ 1) for i in range(count) if i ^ 1 < count]
    far_route = []
    for low in range(1, count - 1, 2):
        far_route += [(low, low + 1), (low + 1, low)]
    halos = []
    for index in range(PARTS):
        block = own[index * part : (index + 1) * part]
        top, low = block[:, :2], block[:, own_rows - 2 :]
        near = lax.ppermute(jnp.where(odd, top, low), "strip", near_route)
        far = lax.ppermute(jnp.where(odd, low, top), "strip", far_route)
        halos.append((near, far))
    prepared = prepare_call(
        own, conv_in, conv_mid, gain_in[None], bias_in[None], gain_mid[None], bias_mid[None]
    )
    carried = None
    for index in range(PARTS):
        near, far = halos[index]
        carried = stage(index * part, part, count, lengths, own, near, far, prepared, carried)
    return carried[0][None]


def solution(mesh):
    data = P(("rep", "clip"), None, "strip", None)
    in_specs = (data, P(("rep", "clip")), P(), P(), P(), P(), P(), P())
    return jax.shard_map(local, mesh=mesh, in_specs=in_specs, out_specs=data, check_vma=False)
```

```python
import functools

import jax
import jax.numpy as jnp
from jax import lax
from jax.experimental import pallas as pl
from jax.experimental.pallas import tpu as pltpu
from jax.sharding import PartitionSpec as P

F32 = jnp.float32
BF16 = jnp.bfloat16
SHORT = 12
PARTS = 2
SCALE = 0.5 * 96.0**0.5


def spread_weight(raw_ref, out_ref):
    row = lax.broadcasted_iota(jnp.int32, (96, 256), 0)
    lane = lax.broadcasted_iota(jnp.int32, (96, 256), 1)
    left = jnp.where(row == lane, 1.0, 0.0).astype(BF16)
    right = jnp.where((row == lane - 96) | ((lane >= 192) & (row == lane - 160)), 1.0, 0.0).astype(BF16)
    for lag in range(3):
        for step in range(3):
            raw = raw_ref[lag, step].reshape(288, 96)
            at_left = jnp.dot(raw, left, preferred_element_type=F32)
            at_right = jnp.dot(raw, right, preferred_element_type=F32)
            first = (at_left[96:192] + at_right[0:96]).astype(BF16)
            second = (at_left[192:288] + at_right[96:192]).astype(BF16)
            after = at_right[192:288].astype(BF16)
            prev = at_left[0:96].astype(BF16)
            base = (3 * lag + step) * 384
            out_ref[base : base + 96] = first
            out_ref[base + 96 : base + 128] = second[:32]
            out_ref[base + 128 : base + 224] = after
            out_ref[base + 224 : base + 256] = prev[:32]
            out_ref[base + 256 : base + 320] = second[32:]
            out_ref[base + 320 : base + 384] = prev[32:]


def twice(left, right):
    return jnp.concatenate([left, right, right[:, 32:]], axis=1)


def group_sum():
    row = lax.broadcasted_iota(jnp.int32, (256, 256), 0)
    column = lax.broadcasted_iota(jnp.int32, (256, 256), 1)
    same = (row < 96) == (column < 96)
    return jnp.where(same & (row < 192), 1.0, 0.0).astype(BF16)


def rms_silu(values, gains, summing):
    narrow = (values * values).astype(BF16)
    total = jnp.dot(narrow, summing, preferred_element_type=F32)
    half = values * (lax.rsqrt(total + 96e-06) * gains)
    return half + half * jnp.tanh(half)


def shift_down(block):
    upper, lower = block[..., :8, :], block[..., 8:, :]
    row = lax.broadcasted_iota(jnp.int32, upper.shape, upper.ndim - 2)
    upper, lower = jnp.roll(upper, 1, axis=-2), jnp.roll(lower, 1, axis=-2)
    return jnp.concatenate([jnp.where(row == 0, 0.0, upper), jnp.where(row == 0, upper, lower)], axis=-2)


def shift_up(block):
    upper, lower = block[..., :8, :], block[..., 8:, :]
    row = lax.broadcasted_iota(jnp.int32, upper.shape, upper.ndim - 2)
    upper, lower = jnp.roll(upper, 7, axis=-2), jnp.roll(lower, 7, axis=-2)
    return jnp.concatenate([jnp.where(row == 7, lower, upper), jnp.where(row == 7, 0.0, lower)], axis=-2)


def store_windows(ref, index, act):
    even0, even1 = act[..., 0, :, :128], act[..., 0, :, 128:]
    odd0, odd1 = act[..., 1, :, :128], act[..., 1, :, 128:]
    lane = lax.broadcasted_iota(jnp.int32, even0.shape, even0.ndim - 1)
    mix = jnp.where(lane < 96, odd0, shift_down(odd0))
    tail = jnp.where(lane < 64, even1, shift_down(odd1))
    full = slice(None)
    ref[(*index, 0, full, slice(0, 128))] = even0.astype(BF16)
    ref[(*index, 0, full, slice(128, 256))] = mix.astype(BF16)
    ref[(*index, 0, full, slice(256, 384))] = tail.astype(BF16)
    mix = jnp.where(lane < 96, shift_up(even0), even0)
    tail = jnp.where(lane < 64, odd1, even1)
    ref[(*index, 1, full, slice(0, 128))] = odd0.astype(BF16)
    ref[(*index, 1, full, slice(128, 256))] = mix.astype(BF16)
    ref[(*index, 1, full, slice(256, 384))] = tail.astype(BF16)


def to_pairs(quad):
    x0, x1, x2 = quad[..., :128], quad[..., 128:256], quad[..., 256:]
    r1 = jnp.roll(x1, 64, axis=-1)
    r2 = jnp.roll(x2, 64, axis=-1)
    lane = lax.broadcasted_iota(jnp.int32, x0.shape, x0.ndim - 1)
    low = lane < 64
    even = jnp.concatenate([x0, jnp.where(low, x1, r1)], axis=-1)
    odd = jnp.concatenate([jnp.where(low, r1, r2), jnp.where(low, r2, x2)], axis=-1)
    return jnp.stack([even, odd], axis=-3)


def from_pairs(both):
    even0, even1 = both[..., 0, :, :128], both[..., 0, :, 128:]
    odd0, odd1 = both[..., 1, :, :128], both[..., 1, :, 128:]
    turned = jnp.roll(odd0, 64, axis=-1)
    lane = lax.broadcasted_iota(jnp.int32, even0.shape, even0.ndim - 1)
    low = lane < 64
    return jnp.concatenate([even0, jnp.where(low, even1, turned), jnp.where(low, turned, odd1)], axis=-1)


def to_quads(values, lines_ref, slot, where, quads):
    count = values.shape[0]
    for q in range(quads):
        for v in range(3):
            lane = (3 * q + v) * 128
            lines_ref[slot, v, pl.ds(where * quads + q, count, stride=quads)] = values[:, lane : lane + 128]


def read_quads(lines_ref, slot, rows, quads):
    parts = [lines_ref[slot, v, 0 : rows * quads] for v in range(3)]
    return jnp.concatenate(parts, axis=1).reshape(rows, quads, 384)


def windows_dot(ref, weight, start, frames, row, count):
    windows = []
    for lag in range(3):
        for step in range(3):
            at = row + step
            windows.append(ref[start + lag : start + lag + frames, at : at + count].reshape(frames * count * 32, 384))
    product = jnp.dot(jnp.concatenate(windows, axis=1), weight, preferred_element_type=F32)
    return product.reshape(frames, count, 32, 256)


def prepare(
    own, raw1, raw2, gain1, bias1, gain2, bias2, w1, w2, vectors, first, second, acc, lines_ref
):
    frames, own_rows, width = own.shape
    quads = width // 384
    inner = own_rows - 2
    spread_weight(raw1, w1)
    spread_weight(raw2, w2)
    for index, (source, scale) in enumerate(((gain1, SCALE), (bias1, 1.0), (gain2, SCALE), (bias2, 1.0))):
        line = source[...] * scale
        vectors[index : index + 1] = twice(line, line)
    summing = group_sum()
    first[0:2] = jnp.zeros_like(first[0:2])
    second[0:2] = jnp.zeros_like(second[0:2])

    lines = LINES // own_rows
    for step in range(frames // lines):
        slot = step % UNROLL
        t = step * lines
        to_quads(own[t : t + lines].astype(F32).reshape(LINES, width), lines_ref, slot, 0, quads)
        quad = read_quads(lines_ref, slot, LINES, quads)
        act = rms_silu(to_pairs(quad).reshape(LINES * 32, 256), vectors[0:1], summing)
        store_windows(
            first, (pl.ds(t + 2, lines), pl.ds(0, own_rows)), act.reshape(lines, own_rows, 2, 16, 256)
        )
    weight = w1[...]
    for row in range(inner):
        acc[row] = windows_dot(first, weight, 0, frames, row, 1)

    for t in range(frames):
        middle = jnp.concatenate([acc[row, t] for row in range(inner)], axis=0)
        middle = (middle.reshape(inner * 32, 256) + vectors[1:2]).astype(BF16).astype(F32)
        act = rms_silu(middle, vectors[2:3], summing)
        store_windows(second, (t + 2, pl.ds(0, inner)), act.reshape(inner, 2, 16, 256))


def body(base, frames, own_rows, quads, count, *refs):
    lengths, own, near, far, w1, w2, vectors, first, second = refs[:9]
    carried = refs[9:12] if base else None
    out, carry1, carry2, first_ref, second_ref, acc1, acc2, lines_ref, turn_ref = refs[12 if base else 9 :]
    length = lengths[0]
    place = lax.axis_index("strip")
    odd = place % 2 == 1
    width = own.shape[2]

    @pl.when(base >= length)
    def _():
        out[...] = jnp.zeros_like(out)

    @pl.when(base < length)
    def _():
        first_ref[:, 2 : 2 + own_rows] = first[base : base + frames + 2]
        second_ref[:, 2:own_rows] = second[base : base + frames + 2]
        if base:
            first_ref[0:2, 0:2] = carried[1][:, 0:2]
            first_ref[0:2, 2 + own_rows :] = carried[1][:, 2:4]
            second_ref[0:2, 0:2] = carried[2][:, 0:2]
            second_ref[0:2, own_rows:] = carried[2][:, 2:4]
        else:
            first_ref[0:2, 0:2] = jnp.zeros_like(first_ref[0:2, 0:2])
            first_ref[0:2, 2 + own_rows :] = jnp.zeros_like(first_ref[0:2, 0:2])
            second_ref[0:2, 0:2] = jnp.zeros_like(second_ref[0:2, 0:2])
            second_ref[0:2, own_rows:] = jnp.zeros_like(second_ref[0:2, 0:2])
        summing = group_sum()
        above = (place > 0).astype(F32)
        below = (place < count - 1).astype(F32)
        near_at = jnp.where(odd, 0, 2 + own_rows)
        far_at = jnp.where(odd, 2 + own_rows, 0)
        each = own_rows // 2
        sub = frames // GROUPS

        def norm1(group):
            lines = LINES // 2
            for step in range(group * sub // lines, (group + 1) * sub // lines):
                for slot, (rows, where) in enumerate(((near, near_at), (far, far_at))):
                    slot += 2 * (step % UNROLL)
                    to_quads(rows[step * LINES : (step + 1) * LINES].astype(F32), lines_ref, slot, 0, quads)
                    quad = read_quads(lines_ref, slot, LINES, quads)
                    act = rms_silu(to_pairs(quad).reshape(LINES * 32, 256), vectors[0:1], summing)
                    store_windows(
                        first_ref, (pl.ds(step * lines + 2, lines), pl.ds(where, 2)), act.reshape(lines, 2, 2, 16, 256)
                    )

        def conv1(group):
            acc1[group, 0] = windows_dot(first_ref, w1[...], group * sub, sub, 0, 2)
            acc1[group, 1] = windows_dot(first_ref, w1[...], group * sub, sub, own_rows, 2)

        def norm2(group):
            for i in range(sub):
                t = group * sub + i
                middle = jnp.concatenate([acc1[group, 0, i], acc1[group, 1, i]], axis=0).reshape(4 * 32, 256)
                middle = (middle + vectors[1:2]).astype(BF16).astype(F32)
                act = rms_silu(middle, vectors[2:3], summing).reshape(4, 2, 16, 256)
                store_windows(second_ref, (t + 2, pl.ds(0, 2)), jnp.concatenate([act[0:1] * above, act[1:2]], axis=0))
                store_windows(
                    second_ref,
                    (t + 2, pl.ds(own_rows, 2)),
                    jnp.concatenate([act[2:3], act[3:4] * below], axis=0),
                )

        def conv2(group):
            acc2[group, 0] = windows_dot(second_ref, w2[...], group * sub, sub, 0, each)
            acc2[group, 1] = windows_dot(second_ref, w2[...], group * sub, sub, each, each)

        def finish(group):
            lines = LINES // own_rows
            for i in range(0, sub, lines):
                t = group * sub + i
                slot = (i // lines) % UNROLL
                branch = jnp.concatenate([acc2[group, 0, i : i + lines], acc2[group, 1, i : i + lines]], axis=1)
                branch = branch.reshape(LINES * 32, 256) + vectors[3:4]
                branch = from_pairs(branch.reshape(LINES, 2, 16, 256)).reshape(LINES * quads, 384)
                for v in range(3):
                    turn_ref[slot, v] = branch[:, v * 128 : v * 128 + 128]
                pieces = []
                for q in range(quads):
                    for v in range(3):
                        pieces.append(turn_ref[slot, v, pl.ds(q, LINES, stride=quads)])
                before = own[base + t : base + t + lines].astype(F32).reshape(LINES, width)
                total = (before + jnp.concatenate(pieces, axis=1)).astype(BF16)
                out[t : t + lines] = total.reshape(lines, own_rows, width)

        steps = (norm1, conv1, norm2, conv2, finish)
        for wave in range(GROUPS + len(steps) - 1):
            for index, step in enumerate(steps):
                if 0 <= wave - index < GROUPS:
                    step(wave - index)
        carry1[:, 0:2] = first_ref[frames : frames + 2, 0:2]
        carry1[:, 2:4] = first_ref[frames : frames + 2, 2 + own_rows :]
        carry2[:, 0:2] = second_ref[frames : frames + 2, 0:2]
        carry2[:, 2:4] = second_ref[frames : frames + 2, own_rows:]
        for t in range(frames):

            @pl.when(base + t >= length)
            def _(t=t):
                out[t] = jnp.zeros_like(out[t])


GROUPS = 1
LINES = 8
UNROLL = 2
VMEM_LIMIT = 30 << 20


def whole(array):
    return pl.BlockSpec(memory_space=pltpu.VMEM)


def prepare_call(own, raw1, raw2, gain1, bias1, gain2, bias2):
    frames, own_rows, width = own.shape
    quads = width // 384
    results = [
        jax.ShapeDtypeStruct((3456, 256), BF16),
        jax.ShapeDtypeStruct((3456, 256), BF16),
        jax.ShapeDtypeStruct((8, 256), F32),
        jax.ShapeDtypeStruct((frames + 2, own_rows, 2, quads, 384), BF16),
        jax.ShapeDtypeStruct((frames + 2, own_rows - 2, 2, quads, 384), BF16),
    ]
    operands = (own, raw1, raw2, gain1, bias1, gain2, bias2)
    return pl.pallas_call(
        prepare,
        grid=(1,),
        out_shape=results,
        in_specs=[whole(a) for a in operands],
        out_specs=[whole(a) for a in results],
        scratch_shapes=[
            pltpu.VMEM((own_rows - 2, frames, 1, 32, 256), F32),
            pltpu.VMEM((UNROLL, 3, LINES * quads, 128), F32),
        ],
        compiler_params=pltpu.CompilerParams(
            dimension_semantics=("arbitrary",), vmem_limit_bytes=VMEM_LIMIT
        ),
        cost_estimate=pl.CostEstimate(
            flops=2 * frames * 2 * 32 * 3456 * 256, bytes_accessed=8 << 20, transcendentals=0
        ),
        name="prepare",
    )(*operands)


def stage(base, frames, count, lengths, own, near, far, prepared, carried):
    own_rows, width = own.shape[1:]
    quads = width // 384
    index = base // frames

    def block(array):
        return pl.BlockSpec(
            (frames,) + array.shape[1:],
            lambda i: (index,) + (0,) * (array.ndim - 1),
            pipeline_mode=pl.Buffered(1),
        )

    w1, w2, vectors, first, second = prepared
    rows1, rows0 = own_rows + 2, own_rows + 4
    carry = [jax.ShapeDtypeStruct((2, 4, 2, quads, 384), BF16)] * 2
    operands = [lengths, own, near, far, w1, w2, vectors, first, second]
    in_specs = [pl.BlockSpec(memory_space=pltpu.SMEM)] + [whole(a) for a in operands[1:]]
    aliases = {}
    if base:
        aliases = {len(operands): 0}
        operands += list(carried)
        in_specs += [pl.BlockSpec(memory_space=pl.ANY)] + [whole(a) for a in carry]
    return pl.pallas_call(
        functools.partial(body, base, frames, own_rows, quads, count),
        grid=(1,),
        out_shape=[jax.ShapeDtypeStruct(own.shape, BF16)] + carry,
        in_specs=in_specs,
        out_specs=[block(own)] + [whole(a) for a in carry],
        scratch_shapes=[
            pltpu.VMEM((frames + 2, rows0, 2, quads, 384), BF16),
            pltpu.VMEM((frames + 2, rows1, 2, quads, 384), BF16),
            pltpu.VMEM((GROUPS, 2, frames // GROUPS, 2, 32, 256), F32),
            pltpu.VMEM((GROUPS, 2, frames // GROUPS, own_rows // 2, 32, 256), F32),
            pltpu.VMEM((2 * UNROLL, 3, LINES * quads, 128), F32),
            pltpu.VMEM((UNROLL, 3, LINES * quads, 128), F32),
        ],
        input_output_aliases=aliases,
        compiler_params=pltpu.CompilerParams(
            dimension_semantics=("arbitrary",), vmem_limit_bytes=VMEM_LIMIT
        ),
        cost_estimate=pl.CostEstimate(
            flops=2 * frames * 8 * 32 * 3456 * 256, bytes_accessed=6 << 20, transcendentals=0
        ),
        name=f"stage{index}",
    )(*operands)


def local(clips, lengths, gain_in, conv_in, bias_in, gain_mid, conv_mid, bias_mid):
    own = clips[0]
    frames, own_rows = own.shape[:2]
    part = frames // PARTS
    count = lax.axis_size("strip")
    odd = lax.axis_index("strip") % 2 == 1
    near_route = [(i, i ^ 1) for i in range(count) if i ^ 1 < count]
    far_route = []
    for low in range(1, count - 1, 2):
        far_route += [(low, low + 1), (low + 1, low)]
    halos = []
    for index in range(PARTS):
        block = own[index * part : (index + 1) * part]
        top, low = block[:, :2], block[:, own_rows - 2 :]
        shape = (2 * part, block.shape[2])
        near = lax.ppermute(jnp.where(odd, top, low).reshape(shape), "strip", near_route)
        far = lax.ppermute(jnp.where(odd, low, top).reshape(shape), "strip", far_route)
        halos.append((near, far))
    prepared = prepare_call(
        own, conv_in, conv_mid, gain_in[None], bias_in[None], gain_mid[None], bias_mid[None]
    )
    carried = None
    for index in range(PARTS):
        near, far = halos[index]
        carried = stage(index * part, part, count, lengths, own, near, far, prepared, carried)
    return carried[0][None]


def solution(mesh):
    data = P(("rep", "clip"), None, "strip", None)
    in_specs = (data, P(("rep", "clip")), P(), P(), P(), P(), P(), P())
    return jax.shard_map(local, mesh=mesh, in_specs=in_specs, out_specs=data, check_vma=False)
```

```python
import functools

import jax
import jax.numpy as jnp
from jax import lax
from jax.experimental import pallas as pl
from jax.experimental.pallas import tpu as pltpu
from jax.sharding import PartitionSpec as P

F32 = jnp.float32
BF16 = jnp.bfloat16
SHORT = 12
PARTS = (10, 14)
SCALE = 0.5 * 96.0**0.5


def spread_weight(raw_ref, out_ref):
    row = lax.broadcasted_iota(jnp.int32, (96, 256), 0)
    lane = lax.broadcasted_iota(jnp.int32, (96, 256), 1)
    left = jnp.where(row == lane, 1.0, 0.0).astype(BF16)
    right = jnp.where((row == lane - 96) | ((lane >= 192) & (row == lane - 160)), 1.0, 0.0).astype(BF16)
    for lag in range(3):
        for step in range(3):
            raw = raw_ref[lag, step].reshape(288, 96)
            at_left = jnp.dot(raw, left, preferred_element_type=F32)
            at_right = jnp.dot(raw, right, preferred_element_type=F32)
            first = (at_left[96:192] + at_right[0:96]).astype(BF16)
            second = (at_left[192:288] + at_right[96:192]).astype(BF16)
            after = at_right[192:288].astype(BF16)
            prev = at_left[0:96].astype(BF16)
            base = (3 * lag + step) * 384
            out_ref[base : base + 96] = first
            out_ref[base + 96 : base + 128] = second[:32]
            out_ref[base + 128 : base + 224] = after
            out_ref[base + 224 : base + 256] = prev[:32]
            out_ref[base + 256 : base + 320] = second[32:]
            out_ref[base + 320 : base + 384] = prev[32:]


def twice(left, right):
    return jnp.concatenate([left, right, right[:, 32:]], axis=1)


def group_sum():
    row = lax.broadcasted_iota(jnp.int32, (256, 256), 0)
    column = lax.broadcasted_iota(jnp.int32, (256, 256), 1)
    same = (row < 96) == (column < 96)
    return jnp.where(same & (row < 192), 1.0, 0.0).astype(BF16)


def rms_silu(values, gains, summing):
    narrow = (values * values).astype(BF16)
    total = jnp.dot(narrow, summing, preferred_element_type=F32)
    half = values * (lax.rsqrt(total + 96e-06) * gains)
    return half + half * jnp.tanh(half)


def shift_down(block):
    upper, lower = block[..., :8, :], block[..., 8:, :]
    row = lax.broadcasted_iota(jnp.int32, upper.shape, upper.ndim - 2)
    upper, lower = jnp.roll(upper, 1, axis=-2), jnp.roll(lower, 1, axis=-2)
    return jnp.concatenate([jnp.where(row == 0, 0.0, upper), jnp.where(row == 0, upper, lower)], axis=-2)


def shift_up(block):
    upper, lower = block[..., :8, :], block[..., 8:, :]
    row = lax.broadcasted_iota(jnp.int32, upper.shape, upper.ndim - 2)
    upper, lower = jnp.roll(upper, 7, axis=-2), jnp.roll(lower, 7, axis=-2)
    return jnp.concatenate([jnp.where(row == 7, lower, upper), jnp.where(row == 7, 0.0, lower)], axis=-2)


def store_windows(ref, index, act):
    even0, even1 = act[..., 0, :, :128], act[..., 0, :, 128:]
    odd0, odd1 = act[..., 1, :, :128], act[..., 1, :, 128:]
    lane = lax.broadcasted_iota(jnp.int32, even0.shape, even0.ndim - 1)
    mix = jnp.where(lane < 96, odd0, shift_down(odd0))
    tail = jnp.where(lane < 64, even1, shift_down(odd1))
    full = slice(None)
    ref[(*index, 0, full, slice(0, 128))] = even0.astype(BF16)
    ref[(*index, 0, full, slice(128, 256))] = mix.astype(BF16)
    ref[(*index, 0, full, slice(256, 384))] = tail.astype(BF16)
    mix = jnp.where(lane < 96, shift_up(even0), even0)
    tail = jnp.where(lane < 64, odd1, even1)
    ref[(*index, 1, full, slice(0, 128))] = odd0.astype(BF16)
    ref[(*index, 1, full, slice(128, 256))] = mix.astype(BF16)
    ref[(*index, 1, full, slice(256, 384))] = tail.astype(BF16)


def to_pairs(quad):
    x0, x1, x2 = quad[..., :128], quad[..., 128:256], quad[..., 256:]
    r1 = jnp.roll(x1, 64, axis=-1)
    r2 = jnp.roll(x2, 64, axis=-1)
    lane = lax.broadcasted_iota(jnp.int32, x0.shape, x0.ndim - 1)
    low = lane < 64
    even = jnp.concatenate([x0, jnp.where(low, x1, r1)], axis=-1)
    odd = jnp.concatenate([jnp.where(low, r1, r2), jnp.where(low, r2, x2)], axis=-1)
    return jnp.stack([even, odd], axis=-3)


def from_pairs(both):
    even0, even1 = both[..., 0, :, :128], both[..., 0, :, 128:]
    odd0, odd1 = both[..., 1, :, :128], both[..., 1, :, 128:]
    turned = jnp.roll(odd0, 64, axis=-1)
    lane = lax.broadcasted_iota(jnp.int32, even0.shape, even0.ndim - 1)
    low = lane < 64
    return jnp.concatenate([even0, jnp.where(low, even1, turned), jnp.where(low, turned, odd1)], axis=-1)


def to_quads(values, lines_ref, slot, where, quads):
    count = values.shape[0]
    for q in range(quads):
        for v in range(3):
            lane = (3 * q + v) * 128
            lines_ref[slot, v, pl.ds(where * quads + q, count, stride=quads)] = values[:, lane : lane + 128]


def read_quads(lines_ref, slot, rows, quads):
    parts = [lines_ref[slot, v, 0 : rows * quads] for v in range(3)]
    return jnp.concatenate(parts, axis=1).reshape(rows, quads, 384)


def windows_dot(ref, weight, start, frames, row, count):
    windows = []
    for lag in range(3):
        for step in range(3):
            at = row + step
            windows.append(ref[start + lag : start + lag + frames, at : at + count].reshape(frames * count * 32, 384))
    product = jnp.dot(jnp.concatenate(windows, axis=1), weight, preferred_element_type=F32)
    return product.reshape(frames, count, 32, 256)


def prepare(
    own, raw1, raw2, gain1, bias1, gain2, bias2, w1, w2, vectors, first, second, acc, lines_ref
):
    frames, own_rows, width = own.shape
    quads = width // 384
    inner = own_rows - 2
    spread_weight(raw1, w1)
    spread_weight(raw2, w2)
    for index, (source, scale) in enumerate(((gain1, SCALE), (bias1, 1.0), (gain2, SCALE), (bias2, 1.0))):
        line = source[...] * scale
        vectors[index : index + 1] = twice(line, line)
    summing = group_sum()
    first[0:2] = jnp.zeros_like(first[0:2])
    second[0:2] = jnp.zeros_like(second[0:2])

    lines = LINES // own_rows
    for step in range(frames // lines):
        slot = step % UNROLL
        t = step * lines
        to_quads(own[t : t + lines].astype(F32).reshape(LINES, width), lines_ref, slot, 0, quads)
        quad = read_quads(lines_ref, slot, LINES, quads)
        act = rms_silu(to_pairs(quad).reshape(LINES * 32, 256), vectors[0:1], summing)
        store_windows(
            first, (pl.ds(t + 2, lines), pl.ds(0, own_rows)), act.reshape(lines, own_rows, 2, 16, 256)
        )
    weight = w1[...]
    for row in range(inner):
        acc[row] = windows_dot(first, weight, 0, frames, row, 1)

    for t in range(frames):
        middle = jnp.concatenate([acc[row, t] for row in range(inner)], axis=0)
        middle = (middle.reshape(inner * 32, 256) + vectors[1:2]).astype(BF16).astype(F32)
        act = rms_silu(middle, vectors[2:3], summing)
        store_windows(second, (t + 2, pl.ds(0, inner)), act.reshape(inner, 2, 16, 256))


def body(base, frames, own_rows, quads, count, *refs):
    lengths, own, near, far, w1, w2, vectors, first, second = refs[:9]
    carried = refs[9:12] if base else None
    out, carry1, carry2, first_ref, second_ref, acc1, acc2, lines_ref, turn_ref, out_ref, out_sems = refs[12 if base else 9 :]
    length = lengths[0]
    place = lax.axis_index("strip")
    odd = place % 2 == 1
    width = own.shape[2]

    @pl.when(base >= length)
    def _():
        out_ref[...] = jnp.zeros_like(out_ref)
        blank = pltpu.make_async_copy(out_ref, out.at[base : base + frames], out_sems.at[0])
        blank.start()
        blank.wait()

    @pl.when(base < length)
    def _():
        first_ref[:, 2 : 2 + own_rows] = first[base : base + frames + 2]
        second_ref[:, 2:own_rows] = second[base : base + frames + 2]
        if base:
            first_ref[0:2, 0:2] = carried[1][:, 0:2]
            first_ref[0:2, 2 + own_rows :] = carried[1][:, 2:4]
            second_ref[0:2, 0:2] = carried[2][:, 0:2]
            second_ref[0:2, own_rows:] = carried[2][:, 2:4]
        else:
            first_ref[0:2, 0:2] = jnp.zeros_like(first_ref[0:2, 0:2])
            first_ref[0:2, 2 + own_rows :] = jnp.zeros_like(first_ref[0:2, 0:2])
            second_ref[0:2, 0:2] = jnp.zeros_like(second_ref[0:2, 0:2])
            second_ref[0:2, own_rows:] = jnp.zeros_like(second_ref[0:2, 0:2])
        summing = group_sum()
        above = (place > 0).astype(F32)
        below = (place < count - 1).astype(F32)
        near_at = jnp.where(odd, 0, 2 + own_rows)
        far_at = jnp.where(odd, 2 + own_rows, 0)
        each = own_rows // 2
        sub = frames // GROUPS

        def norm1(group):
            for t in range(group * sub, (group + 1) * sub, 2):
                for slot, (rows, where) in enumerate(((near, near_at), (far, far_at))):
                    slot += t % (2 * UNROLL)
                    to_quads(rows[t].astype(F32), lines_ref, slot, 0, quads)
                    to_quads(rows[t + 1].astype(F32), lines_ref, slot, 2, quads)
                    quad = read_quads(lines_ref, slot, 4, quads)
                    act = rms_silu(to_pairs(quad).reshape(4 * 32, 256), vectors[0:1], summing)
                    store_windows(first_ref, (pl.ds(t + 2, 2), pl.ds(where, 2)), act.reshape(2, 2, 2, 16, 256))

        def conv1(group):
            acc1[group, 0] = windows_dot(first_ref, w1[...], group * sub, sub, 0, 2)
            acc1[group, 1] = windows_dot(first_ref, w1[...], group * sub, sub, own_rows, 2)

        def norm2(group):
            for i in range(sub):
                t = group * sub + i
                middle = jnp.concatenate([acc1[group, 0, i], acc1[group, 1, i]], axis=0).reshape(4 * 32, 256)
                middle = (middle + vectors[1:2]).astype(BF16).astype(F32)
                act = rms_silu(middle, vectors[2:3], summing).reshape(4, 2, 16, 256)
                store_windows(second_ref, (t + 2, pl.ds(0, 2)), jnp.concatenate([act[0:1] * above, act[1:2]], axis=0))
                store_windows(
                    second_ref,
                    (t + 2, pl.ds(own_rows, 2)),
                    jnp.concatenate([act[2:3], act[3:4] * below], axis=0),
                )

        def conv2(group):
            acc2[group, 0] = windows_dot(second_ref, w2[...], group * sub, sub, 0, each)
            acc2[group, 1] = windows_dot(second_ref, w2[...], group * sub, sub, each, each)

        lines = LINES // own_rows

        def write(index):
            span = pl.ds(index * lines, lines)
            return pltpu.make_async_copy(
                out_ref.at[span], out.at[pl.ds(base + index * lines, lines)], out_sems.at[index]
            )

        def finish(group):
            for i in range(0, sub, lines):
                t = group * sub + i
                slot = (i // lines) % UNROLL
                branch = jnp.concatenate([acc2[group, 0, i : i + lines], acc2[group, 1, i : i + lines]], axis=1)
                branch = branch.reshape(LINES * 32, 256) + vectors[3:4]
                branch = from_pairs(branch.reshape(LINES, 2, 16, 256)).reshape(LINES * quads, 384)
                for v in range(3):
                    turn_ref[slot, v] = branch[:, v * 128 : v * 128 + 128]
                pieces = []
                for q in range(quads):
                    for v in range(3):
                        pieces.append(turn_ref[slot, v, pl.ds(q, LINES, stride=quads)])
                before = own[base + t : base + t + lines].astype(F32).reshape(LINES, width)
                total = before + jnp.concatenate(pieces, axis=1)
                frame = base + t + lax.broadcasted_iota(jnp.int32, total.shape, 0) // own_rows
                total = jnp.where(frame < length, total, 0.0).astype(BF16)
                out_ref[t : t + lines] = total.reshape(lines, own_rows, width)
                write(t // lines).start()

        steps = (norm1, conv1, norm2, conv2, finish)
        for wave in range(GROUPS + len(steps) - 1):
            for index, step in enumerate(steps):
                if 0 <= wave - index < GROUPS:
                    step(wave - index)
        carry1[:, 0:2] = first_ref[frames : frames + 2, 0:2]
        carry1[:, 2:4] = first_ref[frames : frames + 2, 2 + own_rows :]
        carry2[:, 0:2] = second_ref[frames : frames + 2, 0:2]
        carry2[:, 2:4] = second_ref[frames : frames + 2, own_rows:]
        for index in range(frames // lines):
            write(index).wait()


GROUPS = 1
LINES = 8
UNROLL = 2
VMEM_LIMIT = 30 << 20


def whole(array):
    return pl.BlockSpec(memory_space=pltpu.VMEM)


def prepare_call(own, raw1, raw2, gain1, bias1, gain2, bias2):
    frames, own_rows, width = own.shape
    quads = width // 384
    results = [
        jax.ShapeDtypeStruct((3456, 256), BF16),
        jax.ShapeDtypeStruct((3456, 256), BF16),
        jax.ShapeDtypeStruct((8, 256), F32),
        jax.ShapeDtypeStruct((frames + 2, own_rows, 2, quads, 384), BF16),
        jax.ShapeDtypeStruct((frames + 2, own_rows - 2, 2, quads, 384), BF16),
    ]
    operands = (own, raw1, raw2, gain1, bias1, gain2, bias2)
    return pl.pallas_call(
        prepare,
        grid=(1,),
        out_shape=results,
        in_specs=[whole(a) for a in operands],
        out_specs=[whole(a) for a in results],
        scratch_shapes=[
            pltpu.VMEM((own_rows - 2, frames, 1, 32, 256), F32),
            pltpu.VMEM((UNROLL, 3, LINES * quads, 128), F32),
        ],
        compiler_params=pltpu.CompilerParams(
            dimension_semantics=("arbitrary",), vmem_limit_bytes=VMEM_LIMIT
        ),
        cost_estimate=pl.CostEstimate(
            flops=2 * frames * 2 * 32 * 3456 * 256, bytes_accessed=8 << 20, transcendentals=0
        ),
        name="prepare",
    )(*operands)


def stage(base, frames, count, lengths, own, near, far, prepared, carried):
    own_rows, width = own.shape[1:]
    quads = width // 384
    w1, w2, vectors, first, second = prepared
    rows1, rows0 = own_rows + 2, own_rows + 4
    carry = [jax.ShapeDtypeStruct((2, 4, 2, quads, 384), BF16)] * 2
    operands = [lengths, own, near, far, w1, w2, vectors, first, second]
    in_specs = [pl.BlockSpec(memory_space=pltpu.SMEM)] + [whole(a) for a in operands[1:]]
    aliases = {}
    if base:
        aliases = {len(operands): 0}
        operands += list(carried)
        in_specs += [pl.BlockSpec(memory_space=pl.ANY)] + [whole(a) for a in carry]
    return pl.pallas_call(
        functools.partial(body, base, frames, own_rows, quads, count),
        grid=(1,),
        out_shape=[jax.ShapeDtypeStruct(own.shape, BF16)] + carry,
        in_specs=in_specs,
        out_specs=[pl.BlockSpec(memory_space=pl.ANY)] + [whole(a) for a in carry],
        scratch_shapes=[
            pltpu.VMEM((frames + 2, rows0, 2, quads, 384), BF16),
            pltpu.VMEM((frames + 2, rows1, 2, quads, 384), BF16),
            pltpu.VMEM((GROUPS, 2, frames // GROUPS, 2, 32, 256), F32),
            pltpu.VMEM((GROUPS, 2, frames // GROUPS, own_rows // 2, 32, 256), F32),
            pltpu.VMEM((2 * UNROLL, 3, 4 * quads, 128), F32),
            pltpu.VMEM((UNROLL, 3, LINES * quads, 128), F32),
            pltpu.VMEM((frames, own_rows, width), BF16),
            pltpu.SemaphoreType.DMA((frames * own_rows // LINES,)),
        ],
        input_output_aliases=aliases,
        compiler_params=pltpu.CompilerParams(
            dimension_semantics=("arbitrary",), vmem_limit_bytes=VMEM_LIMIT
        ),
        cost_estimate=pl.CostEstimate(
            flops=2 * frames * 8 * 32 * 3456 * 256, bytes_accessed=6 << 20, transcendentals=0
        ),
        name=f"stage{base}",
    )(*operands)


def local(clips, lengths, gain_in, conv_in, bias_in, gain_mid, conv_mid, bias_mid):
    own = clips[0]
    own_rows = own.shape[1]
    count = lax.axis_size("strip")
    odd = lax.axis_index("strip") % 2 == 1
    near_route = [(i, i ^ 1) for i in range(count) if i ^ 1 < count]
    far_route = []
    for low in range(1, count - 1, 2):
        far_route += [(low, low + 1), (low + 1, low)]
    starts = [sum(PARTS[:index]) for index in range(len(PARTS))]
    sends = []
    for start, part in zip(starts, PARTS):
        block = own[start : start + part]
        top, low = block[:, :2], block[:, own_rows - 2 :]
        sends.append((jnp.where(odd, top, low), jnp.where(odd, low, top)))

    def exchange(pair):
        return lax.ppermute(pair[0], "strip", near_route), lax.ppermute(pair[1], "strip", far_route)

    halos = [exchange(sends[0])]
    prepared = prepare_call(
        own, conv_in, conv_mid, gain_in[None], bias_in[None], gain_mid[None], bias_mid[None]
    )
    late, prepared = lax.optimization_barrier((sends[1:], prepared))
    halos += [exchange(pair) for pair in late]
    carried = None
    for index, (start, part) in enumerate(zip(starts, PARTS)):
        near, far = halos[index]
        carried = stage(start, part, count, lengths, own, near, far, prepared, carried)
    return carried[0][None]


def solution(mesh):
    data = P(("rep", "clip"), None, "strip", None)
    in_specs = (data, P(("rep", "clip")), P(), P(), P(), P(), P(), P())
    return jax.shard_map(local, mesh=mesh, in_specs=in_specs, out_specs=data, check_vma=False)
```

```python
import functools

import jax
import jax.numpy as jnp
from jax import lax
from jax.experimental import pallas as pl
from jax.experimental.pallas import tpu as pltpu
from jax.sharding import PartitionSpec as P

F32 = jnp.float32
BF16 = jnp.bfloat16
SHORT = 12
PARTS = (10, 14)
SCALE = 0.5 * 96.0**0.5


def spread_weight(raw_ref, out_ref):
    row = lax.broadcasted_iota(jnp.int32, (96, 256), 0)
    lane = lax.broadcasted_iota(jnp.int32, (96, 256), 1)
    left = jnp.where(row == lane, 1.0, 0.0).astype(BF16)
    right = jnp.where((row == lane - 96) | ((lane >= 192) & (row == lane - 160)), 1.0, 0.0).astype(BF16)
    for lag in range(3):
        for step in range(3):
            raw = raw_ref[lag, step].reshape(288, 96)
            at_left = jnp.dot(raw, left, preferred_element_type=F32)
            at_right = jnp.dot(raw, right, preferred_element_type=F32)
            first = (at_left[96:192] + at_right[0:96]).astype(BF16)
            second = (at_left[192:288] + at_right[96:192]).astype(BF16)
            after = at_right[192:288].astype(BF16)
            prev = at_left[0:96].astype(BF16)
            base = (3 * lag + step) * 384
            out_ref[base : base + 96] = first
            out_ref[base + 96 : base + 128] = second[:32]
            out_ref[base + 128 : base + 224] = after
            out_ref[base + 224 : base + 256] = prev[:32]
            out_ref[base + 256 : base + 320] = second[32:]
            out_ref[base + 320 : base + 384] = prev[32:]


def twice(left, right):
    return jnp.concatenate([left, right, right[:, 32:]], axis=1)


def group_sum():
    row = lax.broadcasted_iota(jnp.int32, (256, 256), 0)
    column = lax.broadcasted_iota(jnp.int32, (256, 256), 1)
    same = (row < 96) == (column < 96)
    return jnp.where(same & (row < 192), 1.0, 0.0).astype(BF16)


def rms_silu(values, gains, summing):
    narrow = (values * values).astype(BF16)
    total = jnp.dot(narrow, summing, preferred_element_type=F32)
    half = values * (lax.rsqrt(total + 96e-06) * gains)
    return half + half * jnp.tanh(half)


def shift_down(block):
    upper, lower = block[..., :8, :], block[..., 8:, :]
    row = lax.broadcasted_iota(jnp.int32, upper.shape, upper.ndim - 2)
    upper, lower = jnp.roll(upper, 1, axis=-2), jnp.roll(lower, 1, axis=-2)
    return jnp.concatenate([jnp.where(row == 0, 0.0, upper), jnp.where(row == 0, upper, lower)], axis=-2)


def shift_up(block):
    upper, lower = block[..., :8, :], block[..., 8:, :]
    row = lax.broadcasted_iota(jnp.int32, upper.shape, upper.ndim - 2)
    upper, lower = jnp.roll(upper, 7, axis=-2), jnp.roll(lower, 7, axis=-2)
    return jnp.concatenate([jnp.where(row == 7, lower, upper), jnp.where(row == 7, 0.0, lower)], axis=-2)


def store_windows(ref, index, act):
    even0, even1 = act[..., 0, :, :128], act[..., 0, :, 128:]
    odd0, odd1 = act[..., 1, :, :128], act[..., 1, :, 128:]
    lane = lax.broadcasted_iota(jnp.int32, even0.shape, even0.ndim - 1)
    mix = jnp.where(lane < 96, odd0, shift_down(odd0))
    tail = jnp.where(lane < 64, even1, shift_down(odd1))
    full = slice(None)
    ref[(*index, 0, full, slice(0, 128))] = even0.astype(BF16)
    ref[(*index, 0, full, slice(128, 256))] = mix.astype(BF16)
    ref[(*index, 0, full, slice(256, 384))] = tail.astype(BF16)
    mix = jnp.where(lane < 96, shift_up(even0), even0)
    tail = jnp.where(lane < 64, odd1, even1)
    ref[(*index, 1, full, slice(0, 128))] = odd0.astype(BF16)
    ref[(*index, 1, full, slice(128, 256))] = mix.astype(BF16)
    ref[(*index, 1, full, slice(256, 384))] = tail.astype(BF16)


def to_pairs(quad):
    x0, x1, x2 = quad[..., :128], quad[..., 128:256], quad[..., 256:]
    r1 = jnp.roll(x1, 64, axis=-1)
    r2 = jnp.roll(x2, 64, axis=-1)
    lane = lax.broadcasted_iota(jnp.int32, x0.shape, x0.ndim - 1)
    low = lane < 64
    even = jnp.concatenate([x0, jnp.where(low, x1, r1)], axis=-1)
    odd = jnp.concatenate([jnp.where(low, r1, r2), jnp.where(low, r2, x2)], axis=-1)
    return jnp.stack([even, odd], axis=-3)


def from_pairs(both):
    even0, even1 = both[..., 0, :, :128], both[..., 0, :, 128:]
    odd0, odd1 = both[..., 1, :, :128], both[..., 1, :, 128:]
    turned = jnp.roll(odd0, 64, axis=-1)
    lane = lax.broadcasted_iota(jnp.int32, even0.shape, even0.ndim - 1)
    low = lane < 64
    return jnp.concatenate([even0, jnp.where(low, even1, turned), jnp.where(low, turned, odd1)], axis=-1)


def to_quads(values, lines_ref, slot, where, quads):
    count = values.shape[0]
    for q in range(quads):
        for v in range(3):
            lane = (3 * q + v) * 128
            lines_ref[slot, v, pl.ds(where * quads + q, count, stride=quads)] = values[:, lane : lane + 128]


def read_quads(lines_ref, slot, rows, quads):
    parts = [lines_ref[slot, v, 0 : rows * quads] for v in range(3)]
    return jnp.concatenate(parts, axis=1).reshape(rows, quads, 384)


def windows_dot(ref, weight, start, frames, row, count):
    windows = []
    for lag in range(3):
        for step in range(3):
            at = row + step
            windows.append(ref[start + lag : start + lag + frames, at : at + count].reshape(frames * count * 32, 384))
    product = jnp.dot(jnp.concatenate(windows, axis=1), weight, preferred_element_type=F32)
    return product.reshape(frames, count, 32, 256)


def prepare(
    own, raw1, raw2, gain1, bias1, gain2, bias2, w1, w2, vectors, first, second, acc, lines_ref
):
    frames, own_rows, width = own.shape
    quads = width // 384
    inner = own_rows - 2
    spread_weight(raw1, w1)
    spread_weight(raw2, w2)
    for index, (source, scale) in enumerate(((gain1, SCALE), (bias1, 1.0), (gain2, SCALE), (bias2, 1.0))):
        line = source[...] * scale
        vectors[index : index + 1] = twice(line, line)
    summing = group_sum()
    first[0:2] = jnp.zeros_like(first[0:2])
    second[0:2] = jnp.zeros_like(second[0:2])

    lines = LINES // own_rows
    for step in range(frames // lines):
        slot = step % UNROLL
        t = step * lines
        to_quads(own[t : t + lines].astype(F32).reshape(LINES, width), lines_ref, slot, 0, quads)
        quad = read_quads(lines_ref, slot, LINES, quads)
        act = rms_silu(to_pairs(quad).reshape(LINES * 32, 256), vectors[0:1], summing)
        store_windows(
            first, (pl.ds(t + 2, lines), pl.ds(0, own_rows)), act.reshape(lines, own_rows, 2, 16, 256)
        )
    weight = w1[...]
    for row in range(inner):
        acc[row] = windows_dot(first, weight, 0, frames, row, 1)

    for t in range(frames):
        middle = jnp.concatenate([acc[row, t] for row in range(inner)], axis=0)
        middle = (middle.reshape(inner * 32, 256) + vectors[1:2]).astype(BF16).astype(F32)
        act = rms_silu(middle, vectors[2:3], summing)
        store_windows(second, (t + 2, pl.ds(0, inner)), act.reshape(inner, 2, 16, 256))


def body(base, frames, own_rows, quads, count, last, *refs):
    lengths, own, near, far, w1, w2, vectors, first, second = refs[:9]
    carried = refs[9:12] if base else None
    out, carry1, carry2, first_ref, second_ref, acc1, acc2, lines_ref, turn_ref, out_ref, out_sems = refs[12 if base else 9 :]
    total_frames = own.shape[0]
    length = lengths[0]
    place = lax.axis_index("strip")
    odd = place % 2 == 1
    width = own.shape[2]

    def blank_rest():
        done = base + frames
        while done < total_frames:
            span = min(frames, total_frames - done)
            out_ref[0:span] = jnp.zeros((span,) + out_ref.shape[1:], BF16)
            rest = pltpu.make_async_copy(out_ref.at[0:span], out.at[done : done + span], out_sems.at[0])
            rest.start()
            rest.wait()
            done += span

    @pl.when(base >= length)
    def _():
        out_ref[...] = jnp.zeros_like(out_ref)
        blank = pltpu.make_async_copy(out_ref, out.at[base : base + frames], out_sems.at[0])
        blank.start()
        blank.wait()

    @pl.when(base < length)
    def _():
        first_ref[:, 2 : 2 + own_rows] = first[base : base + frames + 2]
        second_ref[:, 2:own_rows] = second[base : base + frames + 2]
        if base:
            first_ref[0:2, 0:2] = carried[1][:, 0:2]
            first_ref[0:2, 2 + own_rows :] = carried[1][:, 2:4]
            second_ref[0:2, 0:2] = carried[2][:, 0:2]
            second_ref[0:2, own_rows:] = carried[2][:, 2:4]
        else:
            first_ref[0:2, 0:2] = jnp.zeros_like(first_ref[0:2, 0:2])
            first_ref[0:2, 2 + own_rows :] = jnp.zeros_like(first_ref[0:2, 0:2])
            second_ref[0:2, 0:2] = jnp.zeros_like(second_ref[0:2, 0:2])
            second_ref[0:2, own_rows:] = jnp.zeros_like(second_ref[0:2, 0:2])
        summing = group_sum()
        above = (place > 0).astype(F32)
        below = (place < count - 1).astype(F32)
        near_at = jnp.where(odd, 0, 2 + own_rows)
        far_at = jnp.where(odd, 2 + own_rows, 0)
        each = own_rows // 2
        sub = frames // GROUPS

        def norm1(group):
            for t in range(group * sub, (group + 1) * sub, 2):
                for slot, (rows, where) in enumerate(((near, near_at), (far, far_at))):
                    slot += t % (2 * UNROLL)
                    to_quads(rows[t].astype(F32), lines_ref, slot, 0, quads)
                    to_quads(rows[t + 1].astype(F32), lines_ref, slot, 2, quads)
                    quad = read_quads(lines_ref, slot, 4, quads)
                    act = rms_silu(to_pairs(quad).reshape(4 * 32, 256), vectors[0:1], summing)
                    store_windows(first_ref, (pl.ds(t + 2, 2), pl.ds(where, 2)), act.reshape(2, 2, 2, 16, 256))

        def conv1(group):
            acc1[group, 0] = windows_dot(first_ref, w1[...], group * sub, sub, 0, 2)
            acc1[group, 1] = windows_dot(first_ref, w1[...], group * sub, sub, own_rows, 2)

        def norm2(group):
            for i in range(sub):
                t = group * sub + i
                middle = jnp.concatenate([acc1[group, 0, i], acc1[group, 1, i]], axis=0).reshape(4 * 32, 256)
                middle = (middle + vectors[1:2]).astype(BF16).astype(F32)
                act = rms_silu(middle, vectors[2:3], summing).reshape(4, 2, 16, 256)
                store_windows(second_ref, (t + 2, pl.ds(0, 2)), jnp.concatenate([act[0:1] * above, act[1:2]], axis=0))
                store_windows(
                    second_ref,
                    (t + 2, pl.ds(own_rows, 2)),
                    jnp.concatenate([act[2:3], act[3:4] * below], axis=0),
                )

        def conv2(group):
            acc2[group, 0] = windows_dot(second_ref, w2[...], group * sub, sub, 0, each)
            acc2[group, 1] = windows_dot(second_ref, w2[...], group * sub, sub, each, each)

        lines = LINES // own_rows

        def write(index):
            span = pl.ds(index * lines, lines)
            return pltpu.make_async_copy(
                out_ref.at[span], out.at[pl.ds(base + index * lines, lines)], out_sems.at[index]
            )

        def finish(group):
            for i in range(0, sub, lines):
                t = group * sub + i
                slot = (i // lines) % UNROLL
                branch = jnp.concatenate([acc2[group, 0, i : i + lines], acc2[group, 1, i : i + lines]], axis=1)
                branch = branch.reshape(LINES * 32, 256) + vectors[3:4]
                branch = from_pairs(branch.reshape(LINES, 2, 16, 256)).reshape(LINES * quads, 384)
                for v in range(3):
                    turn_ref[slot, v] = branch[:, v * 128 : v * 128 + 128]
                pieces = []
                for q in range(quads):
                    for v in range(3):
                        pieces.append(turn_ref[slot, v, pl.ds(q, LINES, stride=quads)])
                before = own[base + t : base + t + lines].astype(F32).reshape(LINES, width)
                total = before + jnp.concatenate(pieces, axis=1)
                frame = base + t + lax.broadcasted_iota(jnp.int32, total.shape, 0) // own_rows
                total = jnp.where(frame < length, total, 0.0).astype(BF16)
                out_ref[t : t + lines] = total.reshape(lines, own_rows, width)
                write(t // lines).start()

        steps = (norm1, conv1, norm2, conv2, finish)
        for wave in range(GROUPS + len(steps) - 1):
            for index, step in enumerate(steps):
                if 0 <= wave - index < GROUPS:
                    step(wave - index)
        carry1[:, 0:2] = first_ref[frames : frames + 2, 0:2]
        carry1[:, 2:4] = first_ref[frames : frames + 2, 2 + own_rows :]
        carry2[:, 0:2] = second_ref[frames : frames + 2, 0:2]
        carry2[:, 2:4] = second_ref[frames : frames + 2, own_rows:]
        for index in range(frames // lines):
            write(index).wait()
        if last:
            blank_rest()


GROUPS = 1
LINES = 8
UNROLL = 2
VMEM_LIMIT = 30 << 20


def whole(array):
    return pl.BlockSpec(memory_space=pltpu.VMEM)


def prepare_call(own, raw1, raw2, gain1, bias1, gain2, bias2):
    frames, own_rows, width = own.shape
    quads = width // 384
    results = [
        jax.ShapeDtypeStruct((3456, 256), BF16),
        jax.ShapeDtypeStruct((3456, 256), BF16),
        jax.ShapeDtypeStruct((8, 256), F32),
        jax.ShapeDtypeStruct((frames + 2, own_rows, 2, quads, 384), BF16),
        jax.ShapeDtypeStruct((frames + 2, own_rows - 2, 2, quads, 384), BF16),
    ]
    operands = (own, raw1, raw2, gain1, bias1, gain2, bias2)
    return pl.pallas_call(
        prepare,
        grid=(1,),
        out_shape=results,
        in_specs=[whole(a) for a in operands],
        out_specs=[whole(a) for a in results],
        scratch_shapes=[
            pltpu.VMEM((own_rows - 2, frames, 1, 32, 256), F32),
            pltpu.VMEM((UNROLL, 3, LINES * quads, 128), F32),
        ],
        compiler_params=pltpu.CompilerParams(
            dimension_semantics=("arbitrary",), vmem_limit_bytes=VMEM_LIMIT
        ),
        cost_estimate=pl.CostEstimate(
            flops=2 * frames * 2 * 32 * 3456 * 256, bytes_accessed=8 << 20, transcendentals=0
        ),
        name="prepare",
    )(*operands)


def stage(base, frames, count, last, lengths, own, near, far, prepared, carried):
    own_rows, width = own.shape[1:]
    quads = width // 384
    w1, w2, vectors, first, second = prepared
    rows1, rows0 = own_rows + 2, own_rows + 4
    carry = [jax.ShapeDtypeStruct((2, 4, 2, quads, 384), BF16)] * 2
    operands = [lengths, own, near, far, w1, w2, vectors, first, second]
    in_specs = [pl.BlockSpec(memory_space=pltpu.SMEM)] + [whole(a) for a in operands[1:]]
    aliases = {}
    if base:
        aliases = {len(operands): 0}
        operands += list(carried)
        in_specs += [pl.BlockSpec(memory_space=pl.ANY)] + [whole(a) for a in carry]
    return pl.pallas_call(
        functools.partial(body, base, frames, own_rows, quads, count, last),
        grid=(1,),
        out_shape=[jax.ShapeDtypeStruct(own.shape, BF16)] + carry,
        in_specs=in_specs,
        out_specs=[pl.BlockSpec(memory_space=pl.ANY)] + [whole(a) for a in carry],
        scratch_shapes=[
            pltpu.VMEM((frames + 2, rows0, 2, quads, 384), BF16),
            pltpu.VMEM((frames + 2, rows1, 2, quads, 384), BF16),
            pltpu.VMEM((GROUPS, 2, frames // GROUPS, 2, 32, 256), F32),
            pltpu.VMEM((GROUPS, 2, frames // GROUPS, own_rows // 2, 32, 256), F32),
            pltpu.VMEM((2 * UNROLL, 3, 4 * quads, 128), F32),
            pltpu.VMEM((UNROLL, 3, LINES * quads, 128), F32),
            pltpu.VMEM((frames, own_rows, width), BF16),
            pltpu.SemaphoreType.DMA((frames * own_rows // LINES,)),
        ],
        input_output_aliases=aliases,
        compiler_params=pltpu.CompilerParams(
            dimension_semantics=("arbitrary",), vmem_limit_bytes=VMEM_LIMIT
        ),
        cost_estimate=pl.CostEstimate(
            flops=2 * frames * 8 * 32 * 3456 * 256, bytes_accessed=6 << 20, transcendentals=0
        ),
        name=f"stage{base}",
    )(*operands)


def strips(own, lengths, parts, weights):
    own_rows = own.shape[1]
    count = lax.axis_size("strip")
    odd = lax.axis_index("strip") % 2 == 1
    near_route = [(i, i ^ 1) for i in range(count) if i ^ 1 < count]
    far_route = []
    for low in range(1, count - 1, 2):
        far_route += [(low, low + 1), (low + 1, low)]
    starts = [sum(parts[:index]) for index in range(len(parts))]
    sends = []
    for start, part in zip(starts, parts):
        block = own[start : start + part]
        top, low = block[:, :2], block[:, own_rows - 2 :]
        sends.append((jnp.where(odd, top, low), jnp.where(odd, low, top)))

    def exchange(pair):
        return lax.ppermute(pair[0], "strip", near_route), lax.ppermute(pair[1], "strip", far_route)

    halos = [exchange(sends[0])]
    prepared = prepare_call(own[: sum(parts)], *weights)
    late, prepared = lax.optimization_barrier((sends[1:], prepared))
    halos += [exchange(pair) for pair in late]
    carried = None
    for index, (start, part) in enumerate(zip(starts, parts)):
        near, far = halos[index]
        carried = stage(start, part, count, index == len(parts) - 1, lengths, own, near, far, prepared, carried)
    return carried[0]


def local(clips, lengths, gain_in, conv_in, bias_in, gain_mid, conv_mid, bias_mid):
    weights = (conv_in, conv_mid, gain_in[None], bias_in[None], gain_mid[None], bias_mid[None])

    def heavy(own, lengths, *weights):
        return strips(own, lengths, PARTS, weights)

    def light(own, lengths, *weights):
        return strips(own, lengths, (SHORT,), weights)

    return lax.cond(lengths[0] > SHORT, heavy, light, clips[0], lengths, *weights)[None]


def solution(mesh):
    data = P(("rep", "clip"), None, "strip", None)
    in_specs = (data, P(("rep", "clip")), P(), P(), P(), P(), P(), P())
    return jax.shard_map(local, mesh=mesh, in_specs=in_specs, out_specs=data, check_vma=False)
```

```python
import functools

import jax
import jax.numpy as jnp
from jax import lax
from jax.experimental import pallas as pl
from jax.experimental.pallas import tpu as pltpu
from jax.sharding import PartitionSpec as P

F32 = jnp.float32
BF16 = jnp.bfloat16
SHORT = 12
FIRST = 10
SCALE = 0.5 * 96.0**0.5


def spread_weight(raw_ref, out_ref):
    row = lax.broadcasted_iota(jnp.int32, (96, 256), 0)
    lane = lax.broadcasted_iota(jnp.int32, (96, 256), 1)
    left = jnp.where(row == lane, 1.0, 0.0).astype(BF16)
    right = jnp.where((row == lane - 96) | ((lane >= 192) & (row == lane - 160)), 1.0, 0.0).astype(BF16)
    for lag in range(3):
        for step in range(3):
            raw = raw_ref[lag, step].reshape(288, 96)
            at_left = jnp.dot(raw, left, preferred_element_type=F32)
            at_right = jnp.dot(raw, right, preferred_element_type=F32)
            first = (at_left[96:192] + at_right[0:96]).astype(BF16)
            second = (at_left[192:288] + at_right[96:192]).astype(BF16)
            after = at_right[192:288].astype(BF16)
            prev = at_left[0:96].astype(BF16)
            base = (3 * lag + step) * 384
            out_ref[base : base + 96] = first
            out_ref[base + 96 : base + 128] = second[:32]
            out_ref[base + 128 : base + 224] = after
            out_ref[base + 224 : base + 256] = prev[:32]
            out_ref[base + 256 : base + 320] = second[32:]
            out_ref[base + 320 : base + 384] = prev[32:]


def twice(left, right):
    return jnp.concatenate([left, right, right[:, 32:]], axis=1)


def group_sum():
    row = lax.broadcasted_iota(jnp.int32, (256, 256), 0)
    column = lax.broadcasted_iota(jnp.int32, (256, 256), 1)
    same = (row < 96) == (column < 96)
    return jnp.where(same & (row < 192), 1.0, 0.0).astype(BF16)


def rms_silu(values, gains, summing):
    narrow = (values * values).astype(BF16)
    total = jnp.dot(narrow, summing, preferred_element_type=F32)
    half = values * (lax.rsqrt(total + 96e-06) * gains)
    return half + half * jnp.tanh(half)


def shift_down(block):
    upper, lower = block[..., :8, :], block[..., 8:, :]
    row = lax.broadcasted_iota(jnp.int32, upper.shape, upper.ndim - 2)
    upper, lower = jnp.roll(upper, 1, axis=-2), jnp.roll(lower, 1, axis=-2)
    return jnp.concatenate([jnp.where(row == 0, 0.0, upper), jnp.where(row == 0, upper, lower)], axis=-2)


def shift_up(block):
    upper, lower = block[..., :8, :], block[..., 8:, :]
    row = lax.broadcasted_iota(jnp.int32, upper.shape, upper.ndim - 2)
    upper, lower = jnp.roll(upper, 7, axis=-2), jnp.roll(lower, 7, axis=-2)
    return jnp.concatenate([jnp.where(row == 7, lower, upper), jnp.where(row == 7, 0.0, lower)], axis=-2)


def store_windows(ref, index, act):
    even0, even1 = act[..., 0, :, :128], act[..., 0, :, 128:]
    odd0, odd1 = act[..., 1, :, :128], act[..., 1, :, 128:]
    lane = lax.broadcasted_iota(jnp.int32, even0.shape, even0.ndim - 1)
    mix = jnp.where(lane < 96, odd0, shift_down(odd0))
    tail = jnp.where(lane < 64, even1, shift_down(odd1))
    full = slice(None)
    ref[(*index, 0, full, slice(0, 128))] = even0.astype(BF16)
    ref[(*index, 0, full, slice(128, 256))] = mix.astype(BF16)
    ref[(*index, 0, full, slice(256, 384))] = tail.astype(BF16)
    mix = jnp.where(lane < 96, shift_up(even0), even0)
    tail = jnp.where(lane < 64, odd1, even1)
    ref[(*index, 1, full, slice(0, 128))] = odd0.astype(BF16)
    ref[(*index, 1, full, slice(128, 256))] = mix.astype(BF16)
    ref[(*index, 1, full, slice(256, 384))] = tail.astype(BF16)


def to_pairs(quad):
    x0, x1, x2 = quad[..., :128], quad[..., 128:256], quad[..., 256:]
    r1 = jnp.roll(x1, 64, axis=-1)
    r2 = jnp.roll(x2, 64, axis=-1)
    lane = lax.broadcasted_iota(jnp.int32, x0.shape, x0.ndim - 1)
    low = lane < 64
    even = jnp.concatenate([x0, jnp.where(low, x1, r1)], axis=-1)
    odd = jnp.concatenate([jnp.where(low, r1, r2), jnp.where(low, r2, x2)], axis=-1)
    return jnp.stack([even, odd], axis=-3)


def from_pairs(both):
    even0, even1 = both[..., 0, :, :128], both[..., 0, :, 128:]
    odd0, odd1 = both[..., 1, :, :128], both[..., 1, :, 128:]
    turned = jnp.roll(odd0, 64, axis=-1)
    lane = lax.broadcasted_iota(jnp.int32, even0.shape, even0.ndim - 1)
    low = lane < 64
    return jnp.concatenate([even0, jnp.where(low, even1, turned), jnp.where(low, turned, odd1)], axis=-1)


def to_quads(values, lines_ref, slot, where, quads):
    count = values.shape[0]
    for q in range(quads):
        for v in range(3):
            lane = (3 * q + v) * 128
            lines_ref[slot, v, pl.ds(where * quads + q, count, stride=quads)] = values[:, lane : lane + 128]


def lines_to_quads(own, t, lines, lines_ref, slot, quads):
    for q in range(quads):
        for v in range(3):
            lane = (3 * q + v) * 128
            tile = own[t : t + lines, :, lane : lane + 128].astype(F32).reshape(LINES, 128)
            lines_ref[slot, v, pl.ds(q, LINES, stride=quads)] = tile


def read_quads(lines_ref, slot, rows, quads):
    parts = [lines_ref[slot, v, 0 : rows * quads] for v in range(3)]
    return jnp.concatenate(parts, axis=1).reshape(rows, quads, 384)


def windows_dot(ref, weight, start, frames, row, count):
    windows = []
    for lag in range(3):
        for step in range(3):
            at = row + step
            windows.append(ref[start + lag : start + lag + frames, at : at + count].reshape(frames * count * 32, 384))
    product = jnp.dot(jnp.concatenate(windows, axis=1), weight, preferred_element_type=F32)
    return product.reshape(frames, count, 32, 256)


def prepare(
    own, raw1, raw2, gain1, bias1, gain2, bias2, w1, w2, vectors, first, second, acc, lines_ref
):
    frames, own_rows, width = own.shape
    quads = width // 384
    inner = own_rows - 2
    spread_weight(raw1, w1)
    spread_weight(raw2, w2)
    for index, (source, scale) in enumerate(((gain1, SCALE), (bias1, 1.0), (gain2, SCALE), (bias2, 1.0))):
        line = source[...] * scale
        vectors[index : index + 1] = twice(line, line)
    summing = group_sum()
    first[0:2] = jnp.zeros_like(first[0:2])
    second[0:2] = jnp.zeros_like(second[0:2])

    lines = LINES // own_rows
    for step in range(frames // lines):
        slot = step % UNROLL
        t = step * lines
        lines_to_quads(own, t, lines, lines_ref, slot, quads)
        quad = read_quads(lines_ref, slot, LINES, quads)
        act = rms_silu(to_pairs(quad).reshape(LINES * 32, 256), vectors[0:1], summing)
        store_windows(
            first, (pl.ds(t + 2, lines), pl.ds(0, own_rows)), act.reshape(lines, own_rows, 2, 16, 256)
        )
    weight = w1[...]
    for row in range(inner):
        acc[row] = windows_dot(first, weight, 0, frames, row, 1)

    for t in range(frames):
        middle = jnp.concatenate([acc[row, t] for row in range(inner)], axis=0)
        middle = (middle.reshape(inner * 32, 256) + vectors[1:2]).astype(BF16).astype(F32)
        act = rms_silu(middle, vectors[2:3], summing)
        store_windows(second, (t + 2, pl.ds(0, inner)), act.reshape(inner, 2, 16, 256))


def body(base, frames, own_rows, quads, count, last, *refs):
    lengths, own, near, far, w1, w2, vectors, first, second = refs[:9]
    carried = refs[9:12] if base else None
    out, carry1, carry2, first_ref, second_ref, acc1, acc2, lines_ref, turn_ref, out_ref, out_sems = refs[12 if base else 9 :]
    total_frames = own.shape[0]
    length = lengths[0]
    place = lax.axis_index("strip")
    odd = place % 2 == 1
    width = own.shape[2]

    def blank_rest():
        done = base + frames
        while done < total_frames:
            span = min(frames, total_frames - done)
            out_ref[0:span] = jnp.zeros((span,) + out_ref.shape[1:], BF16)
            rest = pltpu.make_async_copy(out_ref.at[0:span], out.at[done : done + span], out_sems.at[0])
            rest.start()
            rest.wait()
            done += span

    @pl.when(base >= length)
    def _():
        out_ref[...] = jnp.zeros_like(out_ref)
        blank = pltpu.make_async_copy(out_ref, out.at[base : base + frames], out_sems.at[0])
        blank.start()
        blank.wait()
        if last:
            blank_rest()

    @pl.when(base < length)
    def _():
        first_ref[:, 2 : 2 + own_rows] = first[base : base + frames + 2]
        second_ref[:, 2:own_rows] = second[base : base + frames + 2]
        if base:
            first_ref[0:2, 0:2] = carried[1][:, 0:2]
            first_ref[0:2, 2 + own_rows :] = carried[1][:, 2:4]
            second_ref[0:2, 0:2] = carried[2][:, 0:2]
            second_ref[0:2, own_rows:] = carried[2][:, 2:4]
        else:
            first_ref[0:2, 0:2] = jnp.zeros_like(first_ref[0:2, 0:2])
            first_ref[0:2, 2 + own_rows :] = jnp.zeros_like(first_ref[0:2, 0:2])
            second_ref[0:2, 0:2] = jnp.zeros_like(second_ref[0:2, 0:2])
            second_ref[0:2, own_rows:] = jnp.zeros_like(second_ref[0:2, 0:2])
        summing = group_sum()
        above = (place > 0).astype(F32)
        below = (place < count - 1).astype(F32)
        near_at = jnp.where(odd, 0, 2 + own_rows)
        far_at = jnp.where(odd, 2 + own_rows, 0)
        each = own_rows // 2
        sub = frames // GROUPS

        def norm1(group):
            for t in range(group * sub, (group + 1) * sub, 2):
                for slot, (rows, where) in enumerate(((near, near_at), (far, far_at))):
                    slot += t % (2 * UNROLL)
                    to_quads(rows[t].astype(F32), lines_ref, slot, 0, quads)
                    to_quads(rows[t + 1].astype(F32), lines_ref, slot, 2, quads)
                    quad = read_quads(lines_ref, slot, 4, quads)
                    act = rms_silu(to_pairs(quad).reshape(4 * 32, 256), vectors[0:1], summing)
                    store_windows(first_ref, (pl.ds(t + 2, 2), pl.ds(where, 2)), act.reshape(2, 2, 2, 16, 256))

        def conv1(group):
            acc1[group, 0] = windows_dot(first_ref, w1[...], group * sub, sub, 0, 2)
            acc1[group, 1] = windows_dot(first_ref, w1[...], group * sub, sub, own_rows, 2)

        def norm2(group):
            for i in range(sub):
                t = group * sub + i
                middle = jnp.concatenate([acc1[group, 0, i], acc1[group, 1, i]], axis=0).reshape(4 * 32, 256)
                middle = (middle + vectors[1:2]).astype(BF16).astype(F32)
                act = rms_silu(middle, vectors[2:3], summing).reshape(4, 2, 16, 256)
                store_windows(second_ref, (t + 2, pl.ds(0, 2)), jnp.concatenate([act[0:1] * above, act[1:2]], axis=0))
                store_windows(
                    second_ref,
                    (t + 2, pl.ds(own_rows, 2)),
                    jnp.concatenate([act[2:3], act[3:4] * below], axis=0),
                )

        def conv2(group):
            acc2[group, 0] = windows_dot(second_ref, w2[...], group * sub, sub, 0, each)
            acc2[group, 1] = windows_dot(second_ref, w2[...], group * sub, sub, each, each)

        lines = LINES // own_rows

        def write(index):
            span = pl.ds(index * lines, lines)
            return pltpu.make_async_copy(
                out_ref.at[span], out.at[pl.ds(base + index * lines, lines)], out_sems.at[index]
            )

        def finish(group):
            for i in range(0, sub, lines):
                t = group * sub + i
                slot = (i // lines) % UNROLL
                branch = jnp.concatenate([acc2[group, 0, i : i + lines], acc2[group, 1, i : i + lines]], axis=1)
                branch = branch.reshape(LINES * 32, 256) + vectors[3:4]
                branch = from_pairs(branch.reshape(LINES, 2, 16, 256)).reshape(LINES * quads, 384)
                for v in range(3):
                    turn_ref[slot, v] = branch[:, v * 128 : v * 128 + 128]
                pieces = []
                for q in range(quads):
                    for v in range(3):
                        pieces.append(turn_ref[slot, v, pl.ds(q, LINES, stride=quads)])
                before = own[base + t : base + t + lines].astype(F32).reshape(LINES, width)
                total = before + jnp.concatenate(pieces, axis=1)
                frame = base + t + lax.broadcasted_iota(jnp.int32, total.shape, 0) // own_rows
                total = jnp.where(frame < length, total, 0.0).astype(BF16)
                out_ref[t : t + lines] = total.reshape(lines, own_rows, width)
                write(t // lines).start()

        steps = (norm1, conv1, norm2, conv2, finish)
        for wave in range(GROUPS + len(steps) - 1):
            for index, step in enumerate(steps):
                if 0 <= wave - index < GROUPS:
                    step(wave - index)
        carry1[:, 0:2] = first_ref[frames : frames + 2, 0:2]
        carry1[:, 2:4] = first_ref[frames : frames + 2, 2 + own_rows :]
        carry2[:, 0:2] = second_ref[frames : frames + 2, 0:2]
        carry2[:, 2:4] = second_ref[frames : frames + 2, own_rows:]
        for index in range(frames // lines):
            write(index).wait()
        if last:
            blank_rest()


GROUPS = 1
LINES = 8
UNROLL = 4
VMEM_LIMIT = 30 << 20


def whole(array):
    return pl.BlockSpec(memory_space=pltpu.VMEM)


def prepare_call(own, raw1, raw2, gain1, bias1, gain2, bias2):
    frames, own_rows, width = own.shape
    quads = width // 384
    results = [
        jax.ShapeDtypeStruct((3456, 256), BF16),
        jax.ShapeDtypeStruct((3456, 256), BF16),
        jax.ShapeDtypeStruct((8, 256), F32),
        jax.ShapeDtypeStruct((frames + 2, own_rows, 2, quads, 384), BF16),
        jax.ShapeDtypeStruct((frames + 2, own_rows - 2, 2, quads, 384), BF16),
    ]
    operands = (own, raw1, raw2, gain1, bias1, gain2, bias2)
    return pl.pallas_call(
        prepare,
        grid=(1,),
        out_shape=results,
        in_specs=[whole(a) for a in operands],
        out_specs=[whole(a) for a in results],
        scratch_shapes=[
            pltpu.VMEM((own_rows - 2, frames, 1, 32, 256), F32),
            pltpu.VMEM((UNROLL, 3, LINES * quads, 128), F32),
        ],
        compiler_params=pltpu.CompilerParams(
            dimension_semantics=("arbitrary",), vmem_limit_bytes=VMEM_LIMIT
        ),
        cost_estimate=pl.CostEstimate(
            flops=2 * frames * 2 * 32 * 3456 * 256, bytes_accessed=8 << 20, transcendentals=0
        ),
        name="prepare",
    )(*operands)


def stage(base, frames, count, last, lengths, own, near, far, prepared, carried):
    own_rows, width = own.shape[1:]
    quads = width // 384
    w1, w2, vectors, first, second = prepared
    rows1, rows0 = own_rows + 2, own_rows + 4
    carry = [jax.ShapeDtypeStruct((2, 4, 2, quads, 384), BF16)] * 2
    operands = [lengths, own, near, far, w1, w2, vectors, first, second]
    in_specs = [pl.BlockSpec(memory_space=pltpu.SMEM)] + [whole(a) for a in operands[1:]]
    aliases = {}
    if base:
        aliases = {len(operands): 0}
        operands += list(carried)
        in_specs += [pl.BlockSpec(memory_space=pl.ANY)] + [whole(a) for a in carry]
    return pl.pallas_call(
        functools.partial(body, base, frames, own_rows, quads, count, last),
        grid=(1,),
        out_shape=[jax.ShapeDtypeStruct(own.shape, BF16)] + carry,
        in_specs=in_specs,
        out_specs=[pl.BlockSpec(memory_space=pl.ANY)] + [whole(a) for a in carry],
        scratch_shapes=[
            pltpu.VMEM((frames + 2, rows0, 2, quads, 384), BF16),
            pltpu.VMEM((frames + 2, rows1, 2, quads, 384), BF16),
            pltpu.VMEM((GROUPS, 2, frames // GROUPS, 2, 32, 256), F32),
            pltpu.VMEM((GROUPS, 2, frames // GROUPS, own_rows // 2, 32, 256), F32),
            pltpu.VMEM((2 * UNROLL, 3, 4 * quads, 128), F32),
            pltpu.VMEM((UNROLL, 3, LINES * quads, 128), F32),
            pltpu.VMEM((frames, own_rows, width), BF16),
            pltpu.SemaphoreType.DMA((frames * own_rows // LINES,)),
        ],
        input_output_aliases=aliases,
        compiler_params=pltpu.CompilerParams(
            dimension_semantics=("arbitrary",), vmem_limit_bytes=VMEM_LIMIT
        ),
        cost_estimate=pl.CostEstimate(
            flops=2 * frames * 8 * 32 * 3456 * 256, bytes_accessed=6 << 20, transcendentals=0
        ),
        name=f"stage{base}",
    )(*operands)


def routes(count):
    near = [(i, i ^ 1) for i in range(count) if i ^ 1 < count]
    far = []
    for low in range(1, count - 1, 2):
        far += [(low, low + 1), (low + 1, low)]
    return near, far


def exchange(pair):
    near, far = routes(lax.axis_size("strip"))
    return lax.ppermute(pair[0], "strip", near), lax.ppermute(pair[1], "strip", far)


def strips(own, lengths, sends, parts, weights):
    count = lax.axis_size("strip")
    halos = [exchange(sends[0])]
    prepared = prepare_call(own[: sum(parts)], *weights)
    late, prepared = lax.optimization_barrier((sends[1], prepared))
    halos.append(exchange(late))
    carried = None
    start = 0
    for index, part in enumerate(parts):
        last = index == len(parts) - 1
        carried = stage(start, part, count, last, lengths, own, *halos[index], prepared, carried)
        start += part
    return carried[0]


def local(clips, lengths, gain_in, conv_in, bias_in, gain_mid, conv_mid, bias_mid):
    weights = (conv_in, conv_mid, gain_in[None], bias_in[None], gain_mid[None], bias_mid[None])
    own = clips[0]
    odd = lax.axis_index("strip") % 2 == 1
    sends = []
    for block in (own[:FIRST], own[FIRST:]):
        top, low = block[:, :2], block[:, own.shape[1] - 2 :]
        sends.append((jnp.where(odd, top, low), jnp.where(odd, low, top)))
    rest = SHORT - FIRST

    def heavy(own, lengths, sends, *weights):
        return strips(own, lengths, sends, (FIRST, own.shape[0] - FIRST), weights)

    def light(own, lengths, sends, *weights):
        sends = (sends[0], tuple(rows[:rest] for rows in sends[1]))
        return strips(own, lengths, sends, (FIRST, rest), weights)

    return lax.cond(lengths[0] > SHORT, heavy, light, own, lengths, tuple(sends), *weights)[None]


def solution(mesh):
    data = P(("rep", "clip"), None, "strip", None)
    in_specs = (data, P(("rep", "clip")), P(), P(), P(), P(), P(), P())
    return jax.shard_map(local, mesh=mesh, in_specs=in_specs, out_specs=data, check_vma=False)
```
